32 devices in a mesh: fsdp: 8 (over z, x), tensor: 2 (over y), dp: 2 (over core).
Axes of the slice: x: 2, y: 2, z: 4, core: 2. Of those that a mesh axis runs over, the one named last changes fastest.
Arguments:
- states: bfloat16 [4096, 4096], P('fsdp', ('tensor', 'dp')), may hold values from -6 to 6
- fresh_rows: bfloat16 [4096, 4096], P('fsdp', ('tensor', 'dp')), may hold values from -6 to 6
- norm_gain: bfloat16 [4096], P(('tensor', 'dp')), may hold values from 0.25 to 1.75
- gate_weight: bfloat16 [4096, 8192], P('fsdp', ('tensor', 'dp')), may hold values from -0.09375 to 0.09375
- up_weight: bfloat16 [4096, 8192], P('fsdp', ('tensor', 'dp')), may hold values from -0.09375 to 0.09375
- down_weight: bfloat16 [8192, 4096], P(('tensor', 'dp'), 'fsdp'), may hold values from -0.09375 to 0.09375
- halted: int32 [64, 64], P('fsdp'), may hold values from 0 to 1, as said below
- refill_index: int32 [64, 64], P('fsdp'), may hold values from 0 to 63, each once within a row
Outputs:
- next_states: bfloat16 [4096, 4096], P('fsdp', ('tensor', 'dp'))
The draws below stay inside these ranges and needn't reach their ends.
Inputs may be any that keep to these rules, and one draw needn't show every extreme that they name: In each aligned block of 512 rows (in row order over all batches) at most 384 rows are running (halted 0), and some block has exactly 384 running rows. Each batch's row of refill_index holds every number of 0 to 63 once.
All inputs are finite; a program needn't handle non-finite values.
Results may differ from the reference program's by a relative error of at most 0.0085.
Values may be sent and summed in bfloat16 or wider, within the bound.
A program may use at most 128 MiB of HBM per device.

```python
import jax
import jax.numpy as jnp
from jax import lax

D = 4096
FF = 8192
BATCH = 64
ROWS_DEV = 512
ACT_MAX = 384
TOKENS = 4096
NBATCH = 64
N_TENSOR = 2
N_DP = 2


def draw_halted(key, part):
    block_count = TOKENS // ROWS_DEV
    key_count = jax.random.fold_in(key, 11)
    key_top = jax.random.fold_in(key, 12)
    key_rank = jax.random.fold_in(key, 13)
    counts = jax.random.randint(key_count, (block_count,), 1, ACT_MAX + 1)
    chosen = jax.random.randint(key_top, (), 0, block_count)
    counts = jnp.where(jnp.arange(block_count) == chosen, ACT_MAX, counts)
    block_keys = jax.random.split(key_rank, block_count)
    rank_table = jax.vmap(lambda single_key: jax.random.permutation(single_key, ROWS_DEV))(block_keys)
    running = rank_table < counts[:, None]
    stopped = 1 - running.astype(jnp.int32)
    return stopped.reshape(TOKENS // BATCH, BATCH).astype(jnp.int32)


def raised(result, own_key, source, target, shards_of, factor):
    def block_of(position):
        return (jnp.arange(result.shape[position]) // (result.shape[position] // shards_of)).reshape((-1,) + (1,) * (result.ndim - 1 - position))

    one_side = jax.random.permutation(own_key, shards_of)[block_of(target)]
    second = (block_of(target) + shards_of // 2) % shards_of
    return jnp.where((block_of(source) == one_side) | (block_of(source) == second), factor * result, result)


def levels(rng, shape, cuts, least, largest):
    level, own = 1.0, jax.random.fold_in(rng, 6)
    for position, parts in cuts:
        draws = jnp.exp(jax.random.uniform(jax.random.fold_in(own, position), (parts,), jnp.float32, least / len(cuts), largest / len(cuts)))
        level = level * jnp.repeat(draws, shape[position] // parts).reshape([-1 if axis == position else 1 for axis in range(len(shape))])
    return level


def noise(own_key, extent, spread, bound, pieces=(), dtype=jnp.bfloat16):
    gain = levels(own_key, extent, pieces, -0.22, 0.18) if pieces else 1.0
    result = jax.random.normal(own_key, extent, jnp.float32) * spread * gain
    return jnp.minimum(jnp.maximum(result, -bound), bound).astype(dtype)


def heavy_noise(rng, shape, scale, most, pieces, heavy, kind=jnp.bfloat16):
    array = scale * jax.random.normal(rng, shape, jnp.float32)
    if pieces:
        array = array * levels(rng, shape, pieces, -0.22, 0.18)
    return jnp.clip(raised(array, jax.random.fold_in(rng, 3), *heavy), -most, most).astype(kind)


def setup_inputs(seed: int = 0) -> dict:
    keys = jax.random.split(jax.random.key(seed), 9)
    states = noise(keys[0], (TOKENS, D), 1.0, 6.0, ((0, 8), (1, 4)))
    fresh_rows = noise(keys[1], (TOKENS, D), 1.0, 6.0, ((0, 8), (1, 4)))
    norm_gain = jnp.clip(1.0 + 0.15 * jax.random.normal(keys[2], (D,), jnp.float32), 0.25, 1.75).astype(jnp.bfloat16)
    gate_weight = noise(keys[3], (D, FF), D ** -0.5, 0.09375, ((0, 8), (1, 4)))
    up_weight = noise(keys[4], (D, FF), D ** -0.5, 0.09375, ((0, 8), (1, 4)))
    down_weight = heavy_noise(keys[5], (FF, D), FF ** -0.5, 0.09375, ((0, 4), (1, 8)), (0, 1, 8, 2.0))
    halted = draw_halted(jax.random.fold_in(keys[8], 71), 0)
    refill_index = jax.vmap(lambda own: jax.random.permutation(own, BATCH))(jax.random.split(keys[7], NBATCH)).reshape((NBATCH, BATCH)).astype(jnp.int32)
    return {"states": states, "fresh_rows": fresh_rows, "norm_gain": norm_gain, "gate_weight": gate_weight, "up_weight": up_weight, "down_weight": down_weight, "halted": halted, "refill_index": refill_index}


norm_eps = 1e-05

def reference(states, fresh_rows, norm_gain, gate_weight, up_weight, down_weight, halted, refill_index):
    widened = states.astype(jnp.float32)
    mean_square = lax.optimization_barrier(jnp.mean(widened * widened, axis=-1, keepdims=True))
    normed = (widened * lax.rsqrt(mean_square + norm_eps) * norm_gain.astype(jnp.float32)).astype(jnp.bfloat16)
    gate_sum = jnp.dot(normed, gate_weight, preferred_element_type=jnp.float32)
    up_sum = jnp.dot(normed, up_weight, preferred_element_type=jnp.float32)
    hidden = (jax.nn.silu(gate_sum) * up_sum).astype(jnp.bfloat16)
    groups = N_TENSOR * N_DP
    group_width = FF // groups
    hidden_groups = hidden.reshape(TOKENS, groups, group_width).transpose(1, 0, 2)
    down_groups = down_weight.reshape(groups, group_width, D)

    def accumulate(running_sum, group_pair):
        hidden_part, weight_part = group_pair
        partial_value = jnp.dot(hidden_part, weight_part, preferred_element_type=jnp.float32)
        rounded = lax.optimization_barrier(partial_value.astype(jnp.bfloat16))
        return (running_sum + rounded.astype(jnp.float32), None)
    update, _ = lax.scan(accumulate, jnp.zeros((TOKENS, D), jnp.float32), (hidden_groups, down_groups))
    fresh_blocks = fresh_rows.reshape(NBATCH, BATCH, D)
    refilled = jax.vmap(lambda block_rows, pick_index: block_rows[pick_index])(fresh_blocks, refill_index)
    refilled = refilled.reshape(TOKENS, D)
    stopped = (halted.reshape(TOKENS) == 1)[:, None]
    computed = (widened + update).astype(jnp.bfloat16)
    return jnp.where(stopped, refilled, computed)
```

```python
import functools

import jax
import jax.numpy as jnp
from jax import lax
from jax.experimental import pallas as pl
from jax.experimental.pallas import tpu as pltpu
from jax.sharding import PartitionSpec as P

MESH = pl.DeviceIdType.MESH
norm_eps = 1e-05


class Plan:
    def __init__(self, mesh, states, gate, down):
        self.F, self.T, self.C = (mesh.shape[axis] for axis in ("fsdp", "tensor", "dp"))
        self.R = min(4, max(1, self.F // 2))
        self.S = self.F // self.R
        self.K = self.T * self.C
        self.unit = self.F // self.K
        self.rows, self.width = states.shape
        self.cap = self.rows * 3 // 4
        self.features = self.width * self.K
        self.fw = gate.shape[0]
        self.hp = gate.shape[1] // self.R
        self.halves = 2 if self.fw % 256 == 0 else 1
        self.pw = self.fw // self.halves
        self.mats = 2 + self.halves
        self.parts = self.unit * self.halves


def block_kernel(
    p,
    pick_row, pick_col, fill_col, states, fresh, gain, gate_w, up_w, down_w,
    out,
    rows, gate_full, up_full, down_full, gate_acc, up_acc, hidden, kept, ms_c, ms_t,
    crecv, yrecv, zrecv, mine,
    local_sem, gz_send, gz_recv, xs_send, xs_recv, rz_send, rz_recv, ry_send, ry_recv,
    rc_send, rc_recv, mc_send, mc_recv, mt_send, mt_recv,
    oc_send, oc_recv, oy_send, oy_recv, oz_send, oz_recv,
):
    R, S, T, C, K = p.R, p.S, p.T, p.C, p.K
    cap, width, fw, hp, pw = p.cap, p.width, p.fw, p.hp, p.pw
    f, t, c = lax.axis_index("fsdp"), lax.axis_index("tensor"), lax.axis_index("dp")
    a, b = f // S, f % S
    me = t * C + c

    def remote(src, dst, send_sem, recv_sem, axis, index):
        return pltpu.make_async_remote_copy(
            src_ref=src, dst_ref=dst, send_sem=send_sem, recv_sem=recv_sem,
            device_id={axis: index}, device_id_type=MESH,
        )

    def when(cond, run):
        if cond is True:
            run()
        else:
            pl.when(cond)(run)

    def both(one, two):
        return two if one is True else jnp.logical_and(one, two)

    sent = []

    def send(make, cond=True, log=None):
        when(cond, lambda: make().start())
        (sent if log is None else log).append((make, cond))

    def near(step):
        return [(a - step, a >= step), (a + step, a + step < R)]

    by_distance = [(a, True)] + [pair for step in range(1, R) for pair in near(step)]
    arrivals = by_distance[1:]

    def source_at(m, to):
        if m < 2:
            return (gate_w, up_w)[m].at[:, pl.ds(pl.multiple_of(to * hp, hp), hp)]
        h = m - 2
        return down_w.at[pl.ds(pl.multiple_of(to * hp, hp), hp), h * pw : (h + 1) * pw]

    def full_at(m, owner):
        if m < 2:
            return (gate_full, up_full)[m].at[pl.ds(pl.multiple_of(owner * fw, fw), fw), :]
        return down_full.at[m - 2, owner]

    def send_z(m):
        for step in range(R - 1, 0, -1):
            for to, cond in near(step):
                send(
                    lambda m=m, to=to: remote(
                        source_at(m, to), full_at(m, f), gz_send.at[m, to], gz_recv.at[m, a],
                        "fsdp", to * S + b,
                    ),
                    cond,
                )

    def wait_z(m, frm):
        place = full_at(m, frm * S + b)
        remote(place, place, gz_send.at[m, frm], gz_recv.at[m, frm], "fsdp", frm * S + b).wait_recv()

    def send_x(m, frm, cond, own=False):
        for step in range(1, S):
            def make(m=m, frm=frm, step=step):
                place = full_at(m, frm * S + b)
                return remote(
                    source_at(m, a) if own else place, place,
                    xs_send.at[m, frm, step], xs_recv.at[m, frm, step],
                    "fsdp", a * S + (b + step) % S,
                )
            send(make, cond)

    def wait_x(m, frm, step):
        owner = (b + S - step) % S
        place = full_at(m, frm * S + owner)
        remote(
            place, place, xs_send.at[m, frm, step], xs_recv.at[m, frm, step], "fsdp", a * S + owner
        ).wait_recv()

    def local(m):
        return pltpu.make_async_copy(source_at(m, a), full_at(m, f), local_sem.at[m])

    def forward_z(m, pairs):
        for frm, cond in pairs:
            when(cond, lambda frm=frm: wait_z(m, frm))
            send_x(m, frm, cond)

    barrier = pltpu.get_barrier_semaphore()
    partners = [("fsdp", ((a + step) % R) * S + b) for step in range(1, R)]
    partners += [("fsdp", a * S + (b + step) % S) for step in range(1, S)]
    partners += [("tensor", (t + step) % T) for step in range(1, T)]
    partners += [("dp", (c + step) % C) for step in range(1, C)]
    for axis, index in partners:
        pl.semaphore_signal(barrier, inc=1, device_id={axis: index}, device_id_type=MESH)
    pl.semaphore_wait(barrier, len(partners))

    send_z(0)
    send_x(0, a, True, own=True)
    for m in range(p.mats):
        local(m).start()

    ids = lax.broadcasted_iota(jnp.int32, (cap, p.rows), 0)
    picker = (ids == pick_row[...]).astype(jnp.bfloat16)
    picked = jnp.dot(picker, states[...], preferred_element_type=jnp.float32)
    kept[...] = picked.astype(jnp.bfloat16)
    ms_c[c] = jnp.broadcast_to(jnp.sum(picked * picked, axis=-1, keepdims=True), (cap, 128))

    def exchange(buffer, own, axis, count, send_sem, recv_sem):
        def copy(step):
            return remote(
                buffer.at[own], buffer.at[own], send_sem.at[step], recv_sem.at[step],
                axis, (own + step) % count,
            )
        for step in range(1, count):
            send(lambda step=step: copy(step))
        for step in range(1, count):
            place = buffer.at[(own + count - step) % count]
            remote(
                place, place, send_sem.at[step], recv_sem.at[step], axis, (own + count - step) % count
            ).wait_recv()
        return functools.reduce(lambda one, two: one + two, [buffer[k] for k in range(count)])

    ms_t[t] = exchange(ms_c, c, "dp", C, mc_send, mc_recv)
    total_square = exchange(ms_t, t, "tensor", T, mt_send, mt_recv)[:, :1]
    scale = lax.rsqrt(total_square / p.features + norm_eps)
    rows[me, a] = (
        kept[...].astype(jnp.float32) * scale * gain[...].astype(jnp.float32)
    ).astype(jnp.bfloat16)

    row_sent = []

    def row_z(slot, move, cond):
        way = 0 if move > 0 else 1
        place = lambda: rows.at[me, slot]
        send(
            lambda: remote(
                place(), place(), rz_send.at[way, slot], rz_recv.at[slot], "fsdp", (a + move) * S + b
            ),
            cond, row_sent,
        )

    def row_wait_z(slot):
        place = rows.at[me, slot]
        remote(place, place, rz_send.at[0, slot], rz_recv.at[slot], "fsdp", ((a + 1) % R) * S + b).wait_recv()

    def row_y(slot, cond):
        for step in range(1, T):
            send(
                lambda step=step: remote(
                    rows.at[me, slot], rows.at[me, slot], ry_send.at[slot, step], ry_recv.at[slot, step],
                    "tensor", (t + step) % T,
                ),
                cond, row_sent,
            )

    def row_c(slot, tstep, cond):
        block = ((t + T - tstep) % T) * C + c
        for step in range(1, C):
            send(
                lambda step=step: remote(
                    rows.at[block, slot], rows.at[block, slot],
                    rc_send.at[slot, tstep, step], rc_recv.at[slot, tstep, step],
                    "dp", (c + step) % C,
                ),
                cond, row_sent,
            )

    def row_step(step):
        for (slot, cond), move in zip(near(step), (1, -1)):
            when(cond, lambda slot=slot: row_wait_z(slot))
            more = (a + 1 < R) if move > 0 else (a > 0)
            row_z(slot, move, both(cond, more))
            row_y(slot, cond)
            row_c(slot, 0, cond)

    row_z(a, 1, a + 1 < R)
    row_z(a, -1, a > 0)
    row_y(a, True)
    row_c(a, 0, True)
    for m in range(1, p.mats):
        send_x(m, a, True, own=True)

    fresh_ids = lax.broadcasted_iota(jnp.int32, (p.rows, p.rows), 1)
    filler = (fresh_ids == fill_col[...]).astype(jnp.bfloat16)
    out[...] = jnp.dot(filler, fresh[...], preferred_element_type=jnp.float32).astype(jnp.bfloat16)

    if R > 1:
        row_step(1)
    send_z(1)
    forward_z(0, near(1) if R > 1 else [])
    for step in range(2, R):
        row_step(step)
        forward_z(0, near(step))
    for h in range(p.halves):
        send_z(2 + h)
    for slot, cond in by_distance:
        for tstep in range(1, T):
            place = lambda: rows.at[((t + T - tstep) % T) * C + c, slot]
            when(
                cond,
                lambda: remote(
                    place(), place(), ry_send.at[slot, tstep], ry_recv.at[slot, tstep],
                    "tensor", (t + T - tstep) % T,
                ).wait_recv(),
            )
            row_c(slot, tstep, cond)
    for slot in range(R):
        for tstep in range(T):
            for step in range(1, C):
                place = rows.at[((t + T - tstep) % T) * C + (c + C - step) % C, slot]
                remote(
                    place, place, rc_send.at[slot, tstep, step], rc_recv.at[slot, tstep, step],
                    "dp", (c + C - step) % C,
                ).wait_recv()

    per_owner = S // p.unit
    for m in range(p.mats):
        local(m).wait()

    def product_block(block, weights, acc, first):
        span = pl.ds(pl.multiple_of(block * width, width), width)

        def body(slot, carry):
            part = jnp.dot(rows[block, slot], weights[span, :], preferred_element_type=jnp.float32)
            acc[slot] = part if first else acc[slot] + part
            return carry

        lax.fori_loop(0, R, body, 0)

    def products(m, weights, acc, pairs):
        for frm, cond in pairs:
            def run(frm=frm, first=cond is True):
                for step in range(1, S):
                    wait_x(m, frm, step)
                for k in range(per_owner):
                    product_block(frm * per_owner + k, weights, acc, first and k == 0)
            when(cond, run)

    products(0, gate_full, gate_acc, by_distance)
    products(1, up_full, up_acc, by_distance[:1])
    for step in range(1, R):
        forward_z(1, near(step))
        if step > 1:
            products(1, up_full, up_acc, near(step - 1))
    if R > 1:
        products(1, up_full, up_acc, near(R - 1))

    def activate(slot, carry):
        gate = gate_acc[slot]
        hidden[slot] = (gate / (1.0 + jnp.exp(-gate)) * up_acc[slot]).astype(jnp.bfloat16)
        return carry

    lax.fori_loop(0, R, activate, 0)
    for make, cond in row_sent:
        when(cond, lambda make=make: make().wait_send())

    def slot_at(index):
        return jnp.where(index % 2 == 0, R - 1 - index // 2, index // 2)

    def column_part(n):
        return n // p.unit, (b + n % p.unit) % p.unit

    def product(n, slot, block):
        h, i = column_part(n)
        return jnp.dot(hidden[slot], down_full[h, block * p.unit + i], preferred_element_type=jnp.float32)

    def stage(n, block, slot):
        return rows.at[block, slot, :, n * pw : (n + 1) * pw]

    def out_c(n, tstep, slot, step):
        return remote(
            stage(n, tstep * (C - 1) + step - 1, slot), crecv.at[n, tstep, slot, step - 1],
            oc_send.at[n, tstep, slot, step - 1], oc_recv.at[n, tstep, slot, step - 1],
            "dp", (c + step) % C,
        )

    def out_y(n, tstep, slot):
        return remote(
            stage(n, T * (C - 1) + tstep, slot), yrecv.at[n, tstep, slot],
            oy_send.at[n, tstep, slot], oy_recv.at[n, tstep, slot],
            "tensor", (t + 1 + tstep) % T,
        )

    def out_z(n, slot):
        to = jnp.where(slot > a, a + 1, a - 1)
        land = jnp.where(slot == a - 1, R, slot)
        return remote(
            stage(n, K - 1, slot), zrecv.at[n, land], oz_send.at[n, slot], oz_recv.at[n, land],
            "fsdp", to * S + b,
        )

    def wait_out_z(n, land):
        place = zrecv.at[n, land]
        remote(place, place, oz_send.at[n, 0], oz_recv.at[n, land], "fsdp", ((a + 1) % R) * S + b).wait_recv()

    def part_a(n):
        h, turn = n // p.unit, n % p.unit
        m = 2 + h
        if turn == 0:
            forward_z(m, arrivals)
        for frm in range(R):
            for step in range(1, S):
                if (step + turn) % p.unit == 0:
                    wait_x(m, frm, step)

        def body(index, carry):
            tstep, slot = index // R, slot_at(index % R)
            for step in range(1, C):
                block = ((t + 1 + tstep) % T) * C + (c + step) % C
                place = stage(n, tstep * (C - 1) + step - 1, slot)
                place[...] = product(n, slot, block).astype(jnp.bfloat16)
                out_c(n, tstep, slot, step).start()
            return carry

        lax.fori_loop(0, T * R, body, 0)

    def chip_sum(n, tstep, slot):
        value = product(n, slot, ((t + 1 + tstep) % T) * C + c)
        for step in range(1, C):
            out_c(n, tstep, slot, step).wait_recv()
            value = value + crecv[n, tstep, slot, step - 1].astype(jnp.float32)
        return value

    def part_b(n):
        def body(index, carry):
            tstep, slot = index // R, slot_at(index % R)
            place = stage(n, T * (C - 1) + tstep, slot)
            place[...] = chip_sum(n, tstep, slot).astype(jnp.bfloat16)
            out_y(n, tstep, slot).start()
            return carry

        lax.fori_loop(0, (T - 1) * R, body, 0)

    def pass_on(n, slot, value):
        place = stage(n, K - 1, slot)
        place[...] = value.astype(jnp.bfloat16)
        out_z(n, slot).start()

    def part_c(n):
        def body(index, carry):
            slot = slot_at(index)
            value = chip_sum(n, T - 1, slot)
            for tstep in range(T - 1):
                out_y(n, tstep, slot).wait_recv()
                value = value + yrecv[n, tstep, slot].astype(jnp.float32)
            mine[n, slot] = value
            head = jnp.logical_or(
                jnp.logical_and(a == 0, slot > a), jnp.logical_and(a == R - 1, slot < a)
            )
            pl.when(head)(lambda: pass_on(n, slot, mine[n, slot]))
            return carry

        lax.fori_loop(0, R, body, 0)

    def part_d(n):
        def body(index, carry):
            slot = slot_at(index)
            middle = jnp.logical_or(
                jnp.logical_and(slot > a, a > 0), jnp.logical_and(slot < a, a < R - 1)
            )

            @pl.when(middle)
            def _():
                wait_out_z(n, slot)
                pass_on(n, slot, mine[n, slot] + zrecv[n, slot].astype(jnp.float32))

            return carry

        lax.fori_loop(0, R, body, 0)
        for cond, land in ((a > 0, a), (a < R - 1, R)):
            @pl.when(cond)
            def _():
                wait_out_z(n, land)
                mine[n, a] = mine[n, a] + zrecv[n, land].astype(jnp.float32)

        h, i = column_part(n)
        columns = pl.ds(pl.multiple_of(i * fw + h * pw, pw), pw)
        settled = (kept[:, columns].astype(jnp.float32) + mine[n, a]).astype(jnp.bfloat16)
        slots = lax.broadcasted_iota(jnp.int32, (p.rows, cap), 1)
        spread = (slots == pick_col[...]).astype(jnp.bfloat16)
        placed = jnp.dot(spread, settled, preferred_element_type=jnp.float32)
        out[:, columns] = (placed + out[:, columns].astype(jnp.float32)).astype(jnp.bfloat16)

    for n in range(p.parts + 2):
        if n < p.parts:
            part_a(n)
            part_b(n)
        if 1 <= n <= p.parts:
            part_c(n - 1)
        if n >= 2:
            part_d(n - 2)

    for make, cond in sent:
        when(cond, lambda make=make: make().wait_send())

    def settle(index, carry):
        n, slot = index // R, index % R
        for tstep in range(T):
            for step in range(1, C):
                place = crecv.at[n, tstep, slot, step - 1]
                remote(
                    place, place, oc_send.at[n, tstep, slot, step - 1],
                    oc_recv.at[n, tstep, slot, step - 1], "dp", (c + step) % C,
                ).wait_send()
        for tstep in range(T - 1):
            place = yrecv.at[n, tstep, slot]
            remote(
                place, place, oy_send.at[n, tstep, slot], oy_recv.at[n, tstep, slot],
                "tensor", (t + 1 + tstep) % T,
            ).wait_send()

        @pl.when(slot != a)
        def _():
            place = zrecv.at[n, slot]
            remote(
                place, place, oz_send.at[n, slot], oz_recv.at[n, slot],
                "fsdp", ((a + 1) % R) * S + b,
            ).wait_send()

        return carry

    lax.fori_loop(0, p.parts * R, settle, 0)


def make_body(mesh):
    def body(states, fresh_rows, norm_gain, gate_weight, up_weight, down_weight, halted, refill_index):
        p = Plan(mesh, states, gate_weight, down_weight)
        R, S, T, C, K = p.R, p.S, p.T, p.C, p.K
        cap, width, fw, hp, pw = p.cap, p.width, p.fw, p.hp, p.pw
        running = halted.reshape(p.rows) == 0
        slot_of = jnp.cumsum(running.astype(jnp.int32)) - 1
        pick = jnp.where(running, slot_of, -1)
        blocks, batch = refill_index.shape
        base = lax.broadcasted_iota(jnp.int32, (blocks, batch), 0) * batch
        fill = jnp.where(running, -1, (base + refill_index).reshape(p.rows))
        bf16, f32 = jnp.bfloat16, jnp.float32
        dma = lambda *shape: pltpu.SemaphoreType.DMA(shape)
        vmem = pl.BlockSpec(memory_space=pltpu.VMEM)
        hbm = pl.BlockSpec(memory_space=pl.ANY)
        return pl.pallas_call(
            functools.partial(block_kernel, p),
            out_shape=jax.ShapeDtypeStruct(states.shape, states.dtype),
            in_specs=[vmem] * 6 + [hbm] * 3,
            out_specs=vmem,
            scratch_shapes=[
                pltpu.VMEM((K, R, cap, width), bf16),
                pltpu.VMEM((p.features, hp), bf16),
                pltpu.VMEM((p.features, hp), bf16),
                pltpu.VMEM((p.halves, p.F, hp, pw), bf16),
                pltpu.VMEM((R, cap, hp), f32),
                pltpu.VMEM((R, cap, hp), f32),
                pltpu.VMEM((R, cap, hp), bf16),
                pltpu.VMEM((cap, width), bf16),
                pltpu.VMEM((C, cap, 128), f32),
                pltpu.VMEM((T, cap, 128), f32),
                pltpu.VMEM((p.parts, T, R, max(1, C - 1), cap, pw), bf16),
                pltpu.VMEM((p.parts, max(1, T - 1), R, cap, pw), bf16),
                pltpu.VMEM((p.parts, R + 1, cap, pw), bf16),
                pltpu.VMEM((p.parts, R, cap, pw), f32),
                dma(p.mats),
                dma(p.mats, R), dma(p.mats, R),
                dma(p.mats, R, S), dma(p.mats, R, S),
                dma(2, R), dma(R),
                dma(R, T), dma(R, T),
                dma(R, T, C), dma(R, T, C),
                dma(C), dma(C), dma(T), dma(T),
                dma(p.parts, T, R, max(1, C - 1)), dma(p.parts, T, R, max(1, C - 1)),
                dma(p.parts, max(1, T - 1), R), dma(p.parts, max(1, T - 1), R),
                dma(p.parts, R), dma(p.parts, R + 1),
            ],
            compiler_params=pltpu.CompilerParams(
                collective_id=0, has_side_effects=True, vmem_limit_bytes=64000 * 1024
            ),
        )(
            pick.reshape(1, p.rows), pick.reshape(p.rows, 1), fill.reshape(p.rows, 1),
            states, fresh_rows, norm_gain.reshape(1, width), gate_weight, up_weight, down_weight,
        )

    return body


def solution(mesh):
    columns = ("tensor", "dp")
    in_specs = (
        P("fsdp", columns),
        P("fsdp", columns),
        P(columns),
        P("fsdp", columns),
        P("fsdp", columns),
        P(columns, "fsdp"),
        P("fsdp", None),
        P("fsdp", None),
    )
    return jax.shard_map(
        make_body(mesh), mesh=mesh, in_specs=in_specs, out_specs=P("fsdp", columns), check_vma=False
    )
```

```python
import functools

import jax
import jax.numpy as jnp
from jax import lax
from jax.experimental import pallas as pl
from jax.experimental.pallas import tpu as pltpu
from jax.sharding import PartitionSpec as P

MESH = pl.DeviceIdType.MESH
norm_eps = 1e-05


class Plan:
    def __init__(self, mesh, states, gate, down):
        self.F, self.T, self.C = (mesh.shape[axis] for axis in ("fsdp", "tensor", "dp"))
        self.R = min(4, max(1, self.F // 2))
        self.S = self.F // self.R
        self.K = self.T * self.C
        self.unit = self.F // self.K
        self.rows, self.width = states.shape
        self.cap = self.rows * 3 // 4
        self.features = self.width * self.K
        self.fw = gate.shape[0]
        self.hp = gate.shape[1] // self.R
        self.halves = 2 if self.fw % 256 == 0 else 1
        self.pw = self.fw // self.halves
        self.mats = 2 + self.halves
        self.parts = self.unit * self.halves


def block_kernel(
    p,
    pick_row, pick_col, fill_col, states, fresh, gain, gate_w, up_w, down_w,
    out,
    rows, gate_full, up_full, down_full, gate_acc, up_acc, hidden, kept, ms_c, ms_t,
    crecv, yrecv, zrecv, mine,
    local_sem, gz_send, gz_recv, xs_send, xs_recv, rz_send, rz_recv, ry_send, ry_recv,
    rc_send, rc_recv, mc_send, mc_recv, mt_send, mt_recv,
    oc_send, oc_recv, oy_send, oy_recv, oz_send, oz_recv,
):
    R, S, T, C, K = p.R, p.S, p.T, p.C, p.K
    cap, width, fw, hp, pw = p.cap, p.width, p.fw, p.hp, p.pw
    f, t, c = lax.axis_index("fsdp"), lax.axis_index("tensor"), lax.axis_index("dp")
    a, b = f // S, f % S
    me = t * C + c

    def remote(src, dst, send_sem, recv_sem, axis, index):
        return pltpu.make_async_remote_copy(
            src_ref=src, dst_ref=dst, send_sem=send_sem, recv_sem=recv_sem,
            device_id={axis: index}, device_id_type=MESH,
        )

    def when(cond, run):
        if cond is True:
            run()
        else:
            pl.when(cond)(run)

    def both(one, two):
        return two if one is True else jnp.logical_and(one, two)

    sent = []

    def send(make, cond=True, log=None):
        when(cond, lambda: make().start())
        (sent if log is None else log).append((make, cond))

    def near(step):
        return [(a - step, a >= step), (a + step, a + step < R)]

    by_distance = [(a, True)] + [pair for step in range(1, R) for pair in near(step)]
    arrivals = by_distance[1:]

    def source_at(m, to):
        if m < 2:
            return (gate_w, up_w)[m].at[:, pl.ds(pl.multiple_of(to * hp, hp), hp)]
        h = m - 2
        return down_w.at[pl.ds(pl.multiple_of(to * hp, hp), hp), h * pw : (h + 1) * pw]

    def full_at(m, owner):
        if m < 2:
            return (gate_full, up_full)[m].at[pl.ds(pl.multiple_of(owner * fw, fw), fw), :]
        return down_full.at[m - 2, owner]

    at_end = jnp.logical_or(a == 0, a == R - 1)

    def send_z(m, steps, where=None):
        for step in steps:
            for to, cond in near(step):
                cond = cond if where is None else jnp.logical_and(cond, where)
                send(
                    lambda m=m, to=to: remote(
                        source_at(m, to), full_at(m, f), gz_send.at[m, to], gz_recv.at[m, a],
                        "fsdp", to * S + b,
                    ),
                    cond,
                )

    def wait_z(m, frm):
        place = full_at(m, frm * S + b)
        remote(place, place, gz_send.at[m, frm], gz_recv.at[m, frm], "fsdp", frm * S + b).wait_recv()

    def send_x(m, frm, cond, own=False):
        for step in range(1, S):
            def make(m=m, frm=frm, step=step):
                place = full_at(m, frm * S + b)
                return remote(
                    source_at(m, a) if own else place, place,
                    xs_send.at[m, frm, step], xs_recv.at[m, frm, step],
                    "fsdp", a * S + (b + step) % S,
                )
            send(make, cond)

    def wait_x(m, frm, step):
        owner = (b + S - step) % S
        place = full_at(m, frm * S + owner)
        remote(
            place, place, xs_send.at[m, frm, step], xs_recv.at[m, frm, step], "fsdp", a * S + owner
        ).wait_recv()

    def local(m):
        return pltpu.make_async_copy(source_at(m, a), full_at(m, f), local_sem.at[m])

    def forward_z(m, pairs):
        for frm, cond in pairs:
            when(cond, lambda frm=frm: wait_z(m, frm))
            send_x(m, frm, cond)

    barrier = pltpu.get_barrier_semaphore()
    partners = [("fsdp", ((a + step) % R) * S + b) for step in range(1, R)]
    partners += [("fsdp", a * S + (b + step) % S) for step in range(1, S)]
    partners += [("tensor", (t + step) % T) for step in range(1, T)]
    partners += [("dp", (c + step) % C) for step in range(1, C)]
    for axis, index in partners:
        pl.semaphore_signal(barrier, inc=1, device_id={axis: index}, device_id_type=MESH)
    pl.semaphore_wait(barrier, len(partners))

    far = list(range(2, R))
    close = range(1, min(R, 2))
    send_z(0, close)
    send_x(0, a, True, own=True)
    for m in range(p.mats):
        local(m).start()

    ids = lax.broadcasted_iota(jnp.int32, (cap, p.rows), 0)
    picker = (ids == pick_row[...]).astype(jnp.bfloat16)
    picked = jnp.dot(picker, states[...], preferred_element_type=jnp.float32)
    kept[...] = picked.astype(jnp.bfloat16)
    ms_c[c] = jnp.broadcast_to(jnp.sum(picked * picked, axis=-1, keepdims=True), (cap, 128))

    def exchange(buffer, own, axis, count, send_sem, recv_sem):
        def copy(step):
            return remote(
                buffer.at[own], buffer.at[own], send_sem.at[step], recv_sem.at[step],
                axis, (own + step) % count,
            )
        for step in range(1, count):
            send(lambda step=step: copy(step))
        for step in range(1, count):
            place = buffer.at[(own + count - step) % count]
            remote(
                place, place, send_sem.at[step], recv_sem.at[step], axis, (own + count - step) % count
            ).wait_recv()
        return functools.reduce(lambda one, two: one + two, [buffer[k] for k in range(count)])

    ms_t[t] = exchange(ms_c, c, "dp", C, mc_send, mc_recv)
    total_square = exchange(ms_t, t, "tensor", T, mt_send, mt_recv)[:, :1]
    scale = lax.rsqrt(total_square / p.features + norm_eps)
    rows[me, a] = (
        kept[...].astype(jnp.float32) * scale * gain[...].astype(jnp.float32)
    ).astype(jnp.bfloat16)

    row_sent = []

    def row_z(slot, move, cond):
        way = 0 if move > 0 else 1
        place = lambda: rows.at[me, slot]
        send(
            lambda: remote(
                place(), place(), rz_send.at[way, slot], rz_recv.at[slot], "fsdp", (a + move) * S + b
            ),
            cond, row_sent,
        )

    def row_wait_z(slot):
        place = rows.at[me, slot]
        remote(place, place, rz_send.at[0, slot], rz_recv.at[slot], "fsdp", ((a + 1) % R) * S + b).wait_recv()

    def row_y(slot, cond):
        for step in range(1, T):
            send(
                lambda step=step: remote(
                    rows.at[me, slot], rows.at[me, slot], ry_send.at[slot, step], ry_recv.at[slot, step],
                    "tensor", (t + step) % T,
                ),
                cond, row_sent,
            )

    def row_c(slot, tstep, cond):
        block = ((t + T - tstep) % T) * C + c
        for step in range(1, C):
            send(
                lambda step=step: remote(
                    rows.at[block, slot], rows.at[block, slot],
                    rc_send.at[slot, tstep, step], rc_recv.at[slot, tstep, step],
                    "dp", (c + step) % C,
                ),
                cond, row_sent,
            )

    def row_step(step):
        for (slot, cond), move in zip(near(step), (1, -1)):
            when(cond, lambda slot=slot: row_wait_z(slot))
            more = (a + 1 < R) if move > 0 else (a > 0)
            row_z(slot, move, both(cond, more))
            row_y(slot, cond)
            row_c(slot, 0, cond)

    row_z(a, 1, a + 1 < R)
    row_z(a, -1, a > 0)
    send_z(1, close, at_end)
    row_y(a, True)
    row_c(a, 0, True)
    for m in range(1, p.mats):
        send_x(m, a, True, own=True)

    fresh_ids = lax.broadcasted_iota(jnp.int32, (p.rows, p.rows), 1)
    filler = (fresh_ids == fill_col[...]).astype(jnp.bfloat16)
    out[...] = jnp.dot(filler, fresh[...], preferred_element_type=jnp.float32).astype(jnp.bfloat16)

    def row_arrive_y(pairs):
        for slot, cond in pairs:
            for tstep in range(1, T):
                place = lambda: rows.at[((t + T - tstep) % T) * C + c, slot]
                when(
                    cond,
                    lambda: remote(
                        place(), place(), ry_send.at[slot, tstep], ry_recv.at[slot, tstep],
                        "tensor", (t + T - tstep) % T,
                    ).wait_recv(),
                )
                row_c(slot, tstep, cond)

    inner = jnp.logical_not(at_end)
    beyond = range(3, R)

    def only(pairs, where):
        return [(frm, both(cond, where)) for frm, cond in pairs]

    def rim(pairs, yes):
        picked = []
        for frm, cond in pairs:
            end = jnp.logical_or(frm == 0, frm == R - 1)
            picked.append((frm, both(cond, end if yes else jnp.logical_not(end))))
        return picked

    for step in range(1, min(R, 3)):
        row_step(step)
        if step == 1:
            forward_z(0, near(1))
    send_z(1, close, inner)
    send_z(0, far, inner)
    send_z(1, far, inner)
    for step in beyond:
        row_step(step)
    send_z(0, far[::-1], at_end)
    send_z(1, far[::-1], at_end)
    for h in range(p.halves):
        send_z(2 + h, close, at_end)
    send_z(2, far, at_end)
    row_arrive_y(by_distance[:3])
    forward_z(0, only(near(2), at_end))
    forward_z(1, only(near(2), at_end))
    forward_z(1, near(1))
    row_arrive_y(by_distance[3:])
    forward_z(0, only(near(2), inner))
    for step in beyond:
        forward_z(0, near(step))
    for slot in range(R):
        for tstep in range(T):
            for step in range(1, C):
                place = rows.at[((t + T - tstep) % T) * C + (c + C - step) % C, slot]
                remote(
                    place, place, rc_send.at[slot, tstep, step], rc_recv.at[slot, tstep, step],
                    "dp", (c + C - step) % C,
                ).wait_recv()
    for h in range(p.halves):
        send_z(2 + h, close, inner)
        send_z(2 + h, far, inner)

    per_owner = S // p.unit
    for m in range(p.mats):
        local(m).wait()

    def product_block(block, weights, acc, first):
        span = pl.ds(pl.multiple_of(block * width, width), width)

        def body(slot, carry):
            part = jnp.dot(rows[block, slot], weights[span, :], preferred_element_type=jnp.float32)
            acc[slot] = part if first else acc[slot] + part
            return carry

        lax.fori_loop(0, R, body, 0)

    def products(m, pairs):
        weights, acc = ((gate_full, gate_acc), (up_full, up_acc))[m]
        for frm, cond in pairs:
            def run(frm=frm, first=cond is True):
                for step in range(1, S):
                    wait_x(m, frm, step)
                for k in range(per_owner):
                    product_block(frm * per_owner + k, weights, acc, first and k == 0)
            when(cond, run)

    products(0, by_distance[:1])
    for step in range(1, R):
        products(0, near(step))
    products(1, by_distance[:1])
    products(1, near(1))
    products(1, only(near(2), at_end))
    forward_z(1, only(near(2), inner))
    products(1, only(near(2), inner))
    for step in beyond:
        forward_z(1, near(step))
    for step in beyond:
        products(1, near(step))

    def activate(slot, carry):
        gate = gate_acc[slot]
        hidden[slot] = (gate / (1.0 + jnp.exp(-gate)) * up_acc[slot]).astype(jnp.bfloat16)
        return carry

    lax.fori_loop(0, R, activate, 0)
    for make, cond in row_sent:
        when(cond, lambda make=make: make().wait_send())

    def slot_at(index):
        return jnp.where(index % 2 == 0, R - 1 - index // 2, index // 2)

    def column_part(n):
        return n // p.unit, (b + n % p.unit) % p.unit

    def product(n, slot, block):
        h, i = column_part(n)
        return jnp.dot(hidden[slot], down_full[h, block * p.unit + i], preferred_element_type=jnp.float32)

    def stage(n, block, slot):
        return rows.at[block, slot, :, n * pw : (n + 1) * pw]

    def out_c(n, tstep, slot, step):
        return remote(
            stage(n, tstep * (C - 1) + step - 1, slot), crecv.at[n, tstep, slot, step - 1],
            oc_send.at[n, tstep, slot, step - 1], oc_recv.at[n, tstep, slot, step - 1],
            "dp", (c + step) % C,
        )

    def out_y(n, tstep, slot):
        return remote(
            stage(n, T * (C - 1) + tstep, slot), yrecv.at[n, tstep, slot],
            oy_send.at[n, tstep, slot], oy_recv.at[n, tstep, slot],
            "tensor", (t + 1 + tstep) % T,
        )

    def out_z(n, slot):
        to = jnp.where(slot > a, a + 1, a - 1)
        land = jnp.where(slot == a - 1, R, slot)
        return remote(
            stage(n, K - 1, slot), zrecv.at[n, land], oz_send.at[n, slot], oz_recv.at[n, land],
            "fsdp", to * S + b,
        )

    def wait_out_z(n, land):
        place = zrecv.at[n, land]
        remote(place, place, oz_send.at[n, 0], oz_recv.at[n, land], "fsdp", ((a + 1) % R) * S + b).wait_recv()

    def part_a(n):
        h, turn = n // p.unit, n % p.unit
        m = 2 + h
        if turn == 0:
            forward_z(m, arrivals)
            if h + 1 < p.halves:
                send_z(m + 1, far, at_end)
        for frm in range(R):
            for step in range(1, S):
                if (step + turn) % p.unit == 0:
                    wait_x(m, frm, step)

        def body(index, carry):
            tstep, slot = index // R, slot_at(index % R)
            for step in range(1, C):
                block = ((t + 1 + tstep) % T) * C + (c + step) % C
                place = stage(n, tstep * (C - 1) + step - 1, slot)
                place[...] = product(n, slot, block).astype(jnp.bfloat16)
                out_c(n, tstep, slot, step).start()
            return carry

        lax.fori_loop(0, T * R, body, 0)

    def chip_sum(n, tstep, slot):
        value = product(n, slot, ((t + 1 + tstep) % T) * C + c)
        for step in range(1, C):
            out_c(n, tstep, slot, step).wait_recv()
            value = value + crecv[n, tstep, slot, step - 1].astype(jnp.float32)
        return value

    def part_b(n, low, high):
        def body(index, carry):
            tstep, slot = index // (high - low), slot_at(low + index % (high - low))
            place = stage(n, T * (C - 1) + tstep, slot)
            place[...] = chip_sum(n, tstep, slot).astype(jnp.bfloat16)
            out_y(n, tstep, slot).start()
            return carry

        if high > low:
            lax.fori_loop(0, (T - 1) * (high - low), body, 0)

    def pass_on(n, slot, value):
        place = stage(n, K - 1, slot)
        place[...] = value.astype(jnp.bfloat16)
        out_z(n, slot).start()

    def part_c(n, low, high):
        def body(index, carry):
            slot = slot_at(index)
            value = chip_sum(n, T - 1, slot)
            for tstep in range(T - 1):
                out_y(n, tstep, slot).wait_recv()
                value = value + yrecv[n, tstep, slot].astype(jnp.float32)
            mine[n, slot] = value
            head = jnp.logical_or(
                jnp.logical_and(a == 0, slot > a), jnp.logical_and(a == R - 1, slot < a)
            )
            pl.when(head)(lambda: pass_on(n, slot, mine[n, slot]))
            return carry

        lax.fori_loop(low, high, body, 0)

    def part_s(n, low, high, hop):
        def body(index, carry):
            slot = slot_at(index)
            up = jnp.logical_and(a == hop, slot > a)
            down = jnp.logical_and(a == R - 1 - hop, slot < a)

            @pl.when(jnp.logical_or(up, down))
            def _():
                wait_out_z(n, slot)
                pass_on(n, slot, mine[n, slot] + zrecv[n, slot].astype(jnp.float32))

            return carry

        lax.fori_loop(low, high, body, 0)

    def part_f(n):
        for cond, land in ((a > 0, a), (a < R - 1, R)):
            @pl.when(cond)
            def _():
                wait_out_z(n, land)
                mine[n, a] = mine[n, a] + zrecv[n, land].astype(jnp.float32)

        h, i = column_part(n)
        columns = pl.ds(pl.multiple_of(i * fw + h * pw, pw), pw)
        settled = (kept[:, columns].astype(jnp.float32) + mine[n, a]).astype(jnp.bfloat16)
        slots = lax.broadcasted_iota(jnp.int32, (p.rows, cap), 1)
        spread = (slots == pick_col[...]).astype(jnp.bfloat16)
        placed = jnp.dot(spread, settled, preferred_element_type=jnp.float32)
        out[:, columns] = (placed + out[:, columns].astype(jnp.float32)).astype(jnp.bfloat16)

    edge = min(2, R)
    groups = [(0, edge)] + ([(edge, R)] if R > edge else [])
    steady = max(0, p.parts - 2)
    units = [(n, *group) for n in range(steady) for group in groups]
    units += [(n, *group) for group in groups for n in range(steady, p.parts)]
    first = len(groups)
    for n in range(p.parts):
        part_a(n)
        part_b(n, 0, R if n < steady else edge)
        if n == 1:
            for unit in units[:first]:
                part_c(*unit)
    for n in range(steady, p.parts):
        part_b(n, edge, R)
    closed = {}
    for index, unit in enumerate(units):
        closed[unit[0]] = index + R - 2
    for index in range(len(units) + R - 2):
        if index < len(units) and (index >= first or p.parts < 2):
            part_c(*units[index])
        for hop in range(1, R - 1):
            if 0 <= index + 1 - hop < len(units):
                part_s(*units[index + 1 - hop], hop)
        for n in range(p.parts):
            if closed[n] == index:
                part_f(n)

    for make, cond in sent:
        when(cond, lambda make=make: make().wait_send())

    def settle(index, carry):
        n, slot = index // R, index % R
        for tstep in range(T):
            for step in range(1, C):
                place = crecv.at[n, tstep, slot, step - 1]
                remote(
                    place, place, oc_send.at[n, tstep, slot, step - 1],
                    oc_recv.at[n, tstep, slot, step - 1], "dp", (c + step) % C,
                ).wait_send()
        for tstep in range(T - 1):
            place = yrecv.at[n, tstep, slot]
            remote(
                place, place, oy_send.at[n, tstep, slot], oy_recv.at[n, tstep, slot],
                "tensor", (t + 1 + tstep) % T,
            ).wait_send()

        @pl.when(slot != a)
        def _():
            place = zrecv.at[n, slot]
            remote(
                place, place, oz_send.at[n, slot], oz_recv.at[n, slot],
                "fsdp", ((a + 1) % R) * S + b,
            ).wait_send()

        return carry

    lax.fori_loop(0, p.parts * R, settle, 0)


def make_body(mesh):
    def body(states, fresh_rows, norm_gain, gate_weight, up_weight, down_weight, halted, refill_index):
        p = Plan(mesh, states, gate_weight, down_weight)
        R, S, T, C, K = p.R, p.S, p.T, p.C, p.K
        cap, width, fw, hp, pw = p.cap, p.width, p.fw, p.hp, p.pw
        running = halted.reshape(p.rows) == 0
        slot_of = jnp.cumsum(running.astype(jnp.int32)) - 1
        pick = jnp.where(running, slot_of, -1)
        blocks, batch = refill_index.shape
        base = lax.broadcasted_iota(jnp.int32, (blocks, batch), 0) * batch
        fill = jnp.where(running, -1, (base + refill_index).reshape(p.rows))
        bf16, f32 = jnp.bfloat16, jnp.float32
        dma = lambda *shape: pltpu.SemaphoreType.DMA(shape)
        vmem = pl.BlockSpec(memory_space=pltpu.VMEM)
        hbm = pl.BlockSpec(memory_space=pl.ANY)
        return pl.pallas_call(
            functools.partial(block_kernel, p),
            out_shape=jax.ShapeDtypeStruct(states.shape, states.dtype),
            in_specs=[vmem] * 6 + [hbm] * 3,
            out_specs=vmem,
            scratch_shapes=[
                pltpu.VMEM((K, R, cap, width), bf16),
                pltpu.VMEM((p.features, hp), bf16),
                pltpu.VMEM((p.features, hp), bf16),
                pltpu.VMEM((p.halves, p.F, hp, pw), bf16),
                pltpu.VMEM((R, cap, hp), f32),
                pltpu.VMEM((R, cap, hp), f32),
                pltpu.VMEM((R, cap, hp), bf16),
                pltpu.VMEM((cap, width), bf16),
                pltpu.VMEM((C, cap, 128), f32),
                pltpu.VMEM((T, cap, 128), f32),
                pltpu.VMEM((p.parts, T, R, max(1, C - 1), cap, pw), bf16),
                pltpu.VMEM((p.parts, max(1, T - 1), R, cap, pw), bf16),
                pltpu.VMEM((p.parts, R + 1, cap, pw), bf16),
                pltpu.VMEM((p.parts, R, cap, pw), f32),
                dma(p.mats),
                dma(p.mats, R), dma(p.mats, R),
                dma(p.mats, R, S), dma(p.mats, R, S),
                dma(2, R), dma(R),
                dma(R, T), dma(R, T),
                dma(R, T, C), dma(R, T, C),
                dma(C), dma(C), dma(T), dma(T),
                dma(p.parts, T, R, max(1, C - 1)), dma(p.parts, T, R, max(1, C - 1)),
                dma(p.parts, max(1, T - 1), R), dma(p.parts, max(1, T - 1), R),
                dma(p.parts, R), dma(p.parts, R + 1),
            ],
            compiler_params=pltpu.CompilerParams(
                collective_id=0, has_side_effects=True, vmem_limit_bytes=64000 * 1024
            ),
        )(
            pick.reshape(1, p.rows), pick.reshape(p.rows, 1), fill.reshape(p.rows, 1),
            states, fresh_rows, norm_gain.reshape(1, width), gate_weight, up_weight, down_weight,
        )

    return body


def solution(mesh):
    columns = ("tensor", "dp")
    in_specs = (
        P("fsdp", columns),
        P("fsdp", columns),
        P(columns),
        P("fsdp", columns),
        P("fsdp", columns),
        P(columns, "fsdp"),
        P("fsdp", None),
        P("fsdp", None),
    )
    return jax.shard_map(
        make_body(mesh), mesh=mesh, in_specs=in_specs, out_specs=P("fsdp", columns), check_vma=False
    )
```

```python
import functools

import jax
import jax.numpy as jnp
from jax import lax
from jax.experimental import pallas as pl
from jax.experimental.pallas import tpu as pltpu
from jax.sharding import PartitionSpec as P

MESH = pl.DeviceIdType.MESH
norm_eps = 1e-05


class Plan:
    def __init__(self, mesh, states, gate, down):
        self.F, self.T, self.C = (mesh.shape[axis] for axis in ("fsdp", "tensor", "dp"))
        self.R = min(4, max(1, self.F // 2))
        self.S = self.F // self.R
        self.K = self.T * self.C
        self.unit = self.F // self.K
        self.rows, self.width = states.shape
        self.cap = self.rows * 3 // 4
        self.features = self.width * self.K
        self.fw = gate.shape[0]
        self.hp = gate.shape[1] // self.R
        self.halves = self.fw // 128
        self.pw = self.fw // self.halves
        self.mats = 2 + self.halves
        self.parts = self.unit * self.halves


def block_kernel(
    p,
    pick_row, pick_col, fill_col, states, fresh, gain, gate_w, up_w, down_w,
    out,
    rows, gate_full, up_full, down_full, gate_acc, up_acc, hidden, kept, ms_c, ms_t,
    crecv, yrecv, zrecv, mine,
    local_sem, gz_send, gz_recv, xs_send, xs_recv, rz_send, rz_recv, ry_send, ry_recv,
    rc_send, rc_recv, mc_send, mc_recv, mt_send, mt_recv,
    oc_send, oc_recv, oy_send, oy_recv, oz_send, oz_recv, pair_sem,
):
    R, S, T, C, K = p.R, p.S, p.T, p.C, p.K
    cap, width, fw, hp, pw = p.cap, p.width, p.fw, p.hp, p.pw
    f, t, c = lax.axis_index("fsdp"), lax.axis_index("tensor"), lax.axis_index("dp")
    a, b = f // S, f % S
    me = t * C + c

    def remote(src, dst, send_sem, recv_sem, axis, index):
        return pltpu.make_async_remote_copy(
            src_ref=src, dst_ref=dst, send_sem=send_sem, recv_sem=recv_sem,
            device_id={axis: index}, device_id_type=MESH,
        )

    def when(cond, run):
        if cond is True:
            run()
        else:
            pl.when(cond)(run)

    def both(one, two):
        return two if one is True else jnp.logical_and(one, two)

    sent = []

    def send(make, cond=True, log=None):
        when(cond, lambda: make().start())
        (sent if log is None else log).append((make, cond))

    def near(step):
        return [(a - step, a >= step), (a + step, a + step < R)]

    by_distance = [(a, True)] + [pair for step in range(1, R) for pair in near(step)]
    arrivals = by_distance[1:]

    def source_at(m, to):
        if m < 2:
            return (gate_w, up_w)[m].at[:, pl.ds(pl.multiple_of(to * hp, hp), hp)]
        h = m - 2
        return down_w.at[pl.ds(pl.multiple_of(to * hp, hp), hp), h * pw : (h + 1) * pw]

    def full_at(m, owner):
        if m < 2:
            return (gate_full, up_full)[m].at[pl.ds(pl.multiple_of(owner * fw, fw), fw), :]
        return down_full.at[m - 2, owner]

    at_end = jnp.logical_or(a == 0, a == R - 1)

    def send_z(m, steps, where=None, choose=None):
        for step in steps:
            for to, cond in near(step):
                cond = cond if where is None else jnp.logical_and(cond, where)
                cond = cond if choose is None else jnp.logical_and(cond, choose(to))
                send(
                    lambda m=m, to=to: remote(
                        source_at(m, to), full_at(m, f), gz_send.at[m, to], gz_recv.at[m, a],
                        "fsdp", to * S + b,
                    ),
                    cond,
                )

    def wait_z(m, frm):
        place = full_at(m, frm * S + b)
        remote(place, place, gz_send.at[m, frm], gz_recv.at[m, frm], "fsdp", frm * S + b).wait_recv()

    def send_x(m, frm, cond, own=False):
        for step in range(1, S):
            def make(m=m, frm=frm, step=step):
                place = full_at(m, frm * S + b)
                return remote(
                    source_at(m, a) if own else place, place,
                    xs_send.at[m, frm, step], xs_recv.at[m, frm, step],
                    "fsdp", a * S + (b + step) % S,
                )
            send(make, cond)

    def wait_x(m, frm, step):
        owner = (b + S - step) % S
        place = full_at(m, frm * S + owner)
        remote(
            place, place, xs_send.at[m, frm, step], xs_recv.at[m, frm, step], "fsdp", a * S + owner
        ).wait_recv()

    def local(m):
        return pltpu.make_async_copy(source_at(m, a), full_at(m, f), local_sem.at[m])

    def forward_z(m, pairs):
        for frm, cond in pairs:
            when(cond, lambda frm=frm: wait_z(m, frm))
            send_x(m, frm, cond)

    barrier = pltpu.get_barrier_semaphore()
    partners = [("fsdp", ((a + step) % R) * S + b) for step in range(1, R)]
    partners += [("fsdp", a * S + (b + step) % S) for step in range(1, S)]
    partners += [("tensor", (t + step) % T) for step in range(1, T)]
    partners += [("dp", (c + step) % C) for step in range(1, C)]
    for axis, index in partners:
        pl.semaphore_signal(barrier, inc=1, device_id={axis: index}, device_id_type=MESH)
    pl.semaphore_wait(barrier, len(partners))

    far = list(range(2, R))
    close = range(1, min(R, 2))
    send_z(0, close)
    send_x(0, a, True, own=True)
    for m in range(p.mats):
        local(m).start()

    ids = lax.broadcasted_iota(jnp.int32, (cap, p.rows), 0)
    picker = (ids == pick_row[...]).astype(jnp.bfloat16)
    picked = jnp.dot(picker, states[...], preferred_element_type=jnp.float32)
    kept[...] = picked.astype(jnp.bfloat16)
    ms_c[c] = jnp.broadcast_to(jnp.sum(picked * picked, axis=-1, keepdims=True), (cap, 128))

    def exchange(buffer, own, axis, count, send_sem, recv_sem):
        def copy(step):
            return remote(
                buffer.at[own], buffer.at[own], send_sem.at[step], recv_sem.at[step],
                axis, (own + step) % count,
            )
        for step in range(1, count):
            send(lambda step=step: copy(step))
        for step in range(1, count):
            place = buffer.at[(own + count - step) % count]
            remote(
                place, place, send_sem.at[step], recv_sem.at[step], axis, (own + count - step) % count
            ).wait_recv()
        return functools.reduce(lambda one, two: one + two, [buffer[k] for k in range(count)])

    ms_t[t] = exchange(ms_c, c, "dp", C, mc_send, mc_recv)
    total_square = exchange(ms_t, t, "tensor", T, mt_send, mt_recv)[:, :1]
    scale = lax.rsqrt(total_square / p.features + norm_eps)
    rows[me, a] = (
        kept[...].astype(jnp.float32) * scale * gain[...].astype(jnp.float32)
    ).astype(jnp.bfloat16)

    row_sent = []

    def row_z(slot, move, cond):
        way = 0 if move > 0 else 1
        place = lambda: rows.at[me, slot]
        send(
            lambda: remote(
                place(), place(), rz_send.at[way, slot], rz_recv.at[slot], "fsdp", (a + move) * S + b
            ),
            cond, row_sent,
        )

    def row_wait_z(slot):
        place = rows.at[me, slot]
        remote(place, place, rz_send.at[0, slot], rz_recv.at[slot], "fsdp", ((a + 1) % R) * S + b).wait_recv()

    def row_y(slot, cond):
        for step in range(1, T):
            send(
                lambda step=step: remote(
                    rows.at[me, slot], rows.at[me, slot], ry_send.at[slot, step], ry_recv.at[slot, step],
                    "tensor", (t + step) % T,
                ),
                cond, row_sent,
            )

    def row_c(slot, tstep, cond):
        block = ((t + T - tstep) % T) * C + c
        for step in range(1, C):
            send(
                lambda step=step: remote(
                    rows.at[block, slot], rows.at[block, slot],
                    rc_send.at[slot, tstep, step], rc_recv.at[slot, tstep, step],
                    "dp", (c + step) % C,
                ),
                cond, row_sent,
            )

    def row_step(step):
        for (slot, cond), move in zip(near(step), (1, -1)):
            when(cond, lambda slot=slot: row_wait_z(slot))
            more = (a + 1 < R) if move > 0 else (a > 0)
            row_z(slot, move, both(cond, more))
            row_y(slot, cond)
            row_c(slot, 0, cond)

    row_z(a, 1, a + 1 < R)
    row_z(a, -1, a > 0)
    send_z(1, close, at_end)
    row_y(a, True)
    row_c(a, 0, True)
    for m in range(1, p.mats):
        send_x(m, a, True, own=True)

    fresh_ids = lax.broadcasted_iota(jnp.int32, (p.rows, p.rows), 1)
    filler = (fresh_ids == fill_col[...]).astype(jnp.bfloat16)
    out[...] = jnp.dot(filler, fresh[...], preferred_element_type=jnp.float32).astype(jnp.bfloat16)

    def row_arrive_y(pairs):
        for slot, cond in pairs:
            for tstep in range(1, T):
                place = lambda: rows.at[((t + T - tstep) % T) * C + c, slot]
                when(
                    cond,
                    lambda: remote(
                        place(), place(), ry_send.at[slot, tstep], ry_recv.at[slot, tstep],
                        "tensor", (t + T - tstep) % T,
                    ).wait_recv(),
                )
                row_c(slot, tstep, cond)

    inner = jnp.logical_not(at_end)
    beyond = range(3, R)

    def only(pairs, where):
        return [(frm, both(cond, where)) for frm, cond in pairs]

    def rim(pairs, yes):
        picked = []
        for frm, cond in pairs:
            end = jnp.logical_or(frm == 0, frm == R - 1)
            picked.append((frm, both(cond, end if yes else jnp.logical_not(end))))
        return picked

    for step in range(1, min(R, 3)):
        row_step(step)
        if step == 1:
            forward_z(0, near(1))
    send_z(1, close, inner, lambda to: jnp.logical_and(to > 0, to < R - 1))
    send_z(0, far, inner)
    send_z(1, far, inner)
    forward_z(0, only(near(2), at_end))
    forward_z(1, only(near(2), at_end))
    if C > 1:
        @pl.when(at_end)
        def _():
            for step in range(1, C):
                pl.semaphore_signal(
                    pair_sem, inc=1, device_id={"dp": (c + step) % C}, device_id_type=MESH
                )
            pl.semaphore_wait(pair_sem, C - 1)

    for m in range(2):
        send_z(m, far[:1], at_end)
    for step in beyond:
        row_step(step)
    for m in range(2):
        send_z(m, beyond, at_end)
    for h in range(p.halves):
        send_z(2 + h, close, at_end)
    send_z(2, far, at_end)
    row_arrive_y(by_distance[:3])
    forward_z(1, only(near(1), inner))
    row_arrive_y(by_distance[3:])
    send_z(1, close, inner, lambda to: jnp.logical_or(to == 0, to == R - 1))
    forward_z(1, only(near(1), at_end))
    forward_z(0, only(near(2), inner))
    for slot in range(R):
        for tstep in range(T):
            for step in range(1, C):
                place = rows.at[((t + T - tstep) % T) * C + (c + C - step) % C, slot]
                remote(
                    place, place, rc_send.at[slot, tstep, step], rc_recv.at[slot, tstep, step],
                    "dp", (c + C - step) % C,
                ).wait_recv()
    for h in range(p.halves):
        send_z(2 + h, close, inner)
        send_z(2 + h, far, inner)

    per_owner = S // p.unit
    for m in range(p.mats):
        local(m).wait()

    def product_block(block, weights, acc, first):
        span = pl.ds(pl.multiple_of(block * width, width), width)

        def body(slot, carry):
            part = jnp.dot(rows[block, slot], weights[span, :], preferred_element_type=jnp.float32)
            acc[slot] = part if first else acc[slot] + part
            return carry

        lax.fori_loop(0, R, body, 0)

    def products(m, pairs):
        weights, acc = ((gate_full, gate_acc), (up_full, up_acc))[m]
        for frm, cond in pairs:
            def run(frm=frm, first=cond is True):
                for step in range(1, S):
                    wait_x(m, frm, step)
                for k in range(per_owner):
                    product_block(frm * per_owner + k, weights, acc, first and k == 0)
            when(cond, run)

    products(0, by_distance[:1])
    products(0, near(1))
    forward_z(1, only(near(2), inner))
    products(0, only(near(2), at_end))
    for step in beyond:
        forward_z(0, near(step))
    products(1, by_distance[:1])
    products(1, only(near(2), at_end))
    products(1, near(1))
    for step in beyond:
        forward_z(1, near(step))
        products(0, near(step))
    products(0, only(near(2), inner))
    products(1, only(near(2), inner))
    for step in beyond:
        products(1, near(step))

    def activate(slot, carry):
        gate = gate_acc[slot]
        hidden[slot] = (gate / (1.0 + jnp.exp(-gate)) * up_acc[slot]).astype(jnp.bfloat16)
        return carry

    lax.fori_loop(0, R, activate, 0)
    for make, cond in row_sent:
        when(cond, lambda make=make: make().wait_send())

    def slot_at(index):
        return jnp.where(index % 2 == 0, R - 1 - index // 2, index // 2)

    def column_part(n):
        return n // p.unit, (b + n % p.unit) % p.unit

    def product(n, slot, block):
        h, i = column_part(n)
        return jnp.dot(hidden[slot], down_full[h, block * p.unit + i], preferred_element_type=jnp.float32)

    def stage(n, block, slot):
        return rows.at[block, slot, :, n * pw : (n + 1) * pw]

    def out_c(n, tstep, slot, step):
        return remote(
            stage(n, tstep * (C - 1) + step - 1, slot), crecv.at[n, tstep, slot, step - 1],
            oc_send.at[n, tstep, slot, step - 1], oc_recv.at[n, tstep, slot, step - 1],
            "dp", (c + step) % C,
        )

    def out_y(n, tstep, slot):
        return remote(
            stage(n, T * (C - 1) + tstep, slot), yrecv.at[n, tstep, slot],
            oy_send.at[n, tstep, slot], oy_recv.at[n, tstep, slot],
            "tensor", (t + 1 + tstep) % T,
        )

    def out_z(n, slot):
        to = jnp.where(slot > a, a + 1, a - 1)
        land = jnp.where(slot == a - 1, R, slot)
        return remote(
            stage(n, K - 1, slot), zrecv.at[n, land], oz_send.at[n, slot], oz_recv.at[n, land],
            "fsdp", to * S + b,
        )

    def wait_out_z(n, land):
        place = zrecv.at[n, land]
        remote(place, place, oz_send.at[n, 0], oz_recv.at[n, land], "fsdp", ((a + 1) % R) * S + b).wait_recv()

    def part_a(n):
        h, turn = n // p.unit, n % p.unit
        m = 2 + h
        if turn == 0:
            forward_z(m, arrivals)
            if h + 1 < p.halves:
                send_z(m + 1, far, at_end)
        for frm in range(R):
            for step in range(1, S):
                if (step + turn) % p.unit == 0:
                    wait_x(m, frm, step)

        def body(index, carry):
            tstep, slot = index // R, slot_at(index % R)
            for step in range(1, C):
                block = ((t + 1 + tstep) % T) * C + (c + step) % C
                place = stage(n, tstep * (C - 1) + step - 1, slot)
                place[...] = product(n, slot, block).astype(jnp.bfloat16)
                out_c(n, tstep, slot, step).start()
            return carry

        lax.fori_loop(0, T * R, body, 0)

    def chip_sum(n, tstep, slot):
        value = product(n, slot, ((t + 1 + tstep) % T) * C + c)
        for step in range(1, C):
            out_c(n, tstep, slot, step).wait_recv()
            value = value + crecv[n, tstep, slot, step - 1].astype(jnp.float32)
        return value

    def part_b(n, low, high):
        def body(index, carry):
            tstep, slot = index // (high - low), slot_at(low + index % (high - low))
            place = stage(n, T * (C - 1) + tstep, slot)
            place[...] = chip_sum(n, tstep, slot).astype(jnp.bfloat16)
            out_y(n, tstep, slot).start()
            return carry

        if high > low:
            lax.fori_loop(0, (T - 1) * (high - low), body, 0)

    def pass_on(n, slot, value):
        place = stage(n, K - 1, slot)
        place[...] = value.astype(jnp.bfloat16)
        out_z(n, slot).start()

    def part_c(n, low, high):
        def body(index, carry):
            slot = slot_at(index)
            value = chip_sum(n, T - 1, slot)
            for tstep in range(T - 1):
                out_y(n, tstep, slot).wait_recv()
                value = value + yrecv[n, tstep, slot].astype(jnp.float32)
            mine[n, slot] = value
            head = jnp.logical_or(
                jnp.logical_and(a == 0, slot > a), jnp.logical_and(a == R - 1, slot < a)
            )
            pl.when(head)(lambda: pass_on(n, slot, mine[n, slot]))
            return carry

        lax.fori_loop(low, high, body, 0)

    def part_s(n, low, high, hop):
        def body(index, carry):
            slot = slot_at(index)
            up = jnp.logical_and(a == hop, slot > a)
            down = jnp.logical_and(a == R - 1 - hop, slot < a)

            @pl.when(jnp.logical_or(up, down))
            def _():
                wait_out_z(n, slot)
                pass_on(n, slot, mine[n, slot] + zrecv[n, slot].astype(jnp.float32))

            return carry

        lax.fori_loop(low, high, body, 0)

    def part_f(n):
        for cond, land in ((a > 0, a), (a < R - 1, R)):
            @pl.when(cond)
            def _():
                wait_out_z(n, land)
                mine[n, a] = mine[n, a] + zrecv[n, land].astype(jnp.float32)

        h, i = column_part(n)
        columns = pl.ds(pl.multiple_of(i * fw + h * pw, pw), pw)
        settled = (kept[:, columns].astype(jnp.float32) + mine[n, a]).astype(jnp.bfloat16)
        slots = lax.broadcasted_iota(jnp.int32, (p.rows, cap), 1)
        spread = (slots == pick_col[...]).astype(jnp.bfloat16)
        placed = jnp.dot(spread, settled, preferred_element_type=jnp.float32)
        out[:, columns] = (placed + out[:, columns].astype(jnp.float32)).astype(jnp.bfloat16)

    behind = 2
    for tick in range(p.parts + behind + R - 1):
        if tick < p.parts:
            part_a(tick)
            part_b(tick, 0, R)
        if 0 <= tick - behind < p.parts:
            part_c(tick - behind, 0, R)
        for hop in range(1, R - 1):
            if 0 <= tick - behind + 1 - hop < p.parts:
                part_s(tick - behind + 1 - hop, 0, R, hop)
        if 0 <= tick - behind - R + 2 < p.parts:
            part_f(tick - behind - R + 2)

    for make, cond in sent:
        when(cond, lambda make=make: make().wait_send())

    def settle(index, carry):
        n, slot = index // R, index % R
        for tstep in range(T):
            for step in range(1, C):
                place = crecv.at[n, tstep, slot, step - 1]
                remote(
                    place, place, oc_send.at[n, tstep, slot, step - 1],
                    oc_recv.at[n, tstep, slot, step - 1], "dp", (c + step) % C,
                ).wait_send()
        for tstep in range(T - 1):
            place = yrecv.at[n, tstep, slot]
            remote(
                place, place, oy_send.at[n, tstep, slot], oy_recv.at[n, tstep, slot],
                "tensor", (t + 1 + tstep) % T,
            ).wait_send()

        @pl.when(slot != a)
        def _():
            place = zrecv.at[n, slot]
            remote(
                place, place, oz_send.at[n, slot], oz_recv.at[n, slot],
                "fsdp", ((a + 1) % R) * S + b,
            ).wait_send()

        return carry

    lax.fori_loop(0, p.parts * R, settle, 0)


def make_body(mesh):
    def body(states, fresh_rows, norm_gain, gate_weight, up_weight, down_weight, halted, refill_index):
        p = Plan(mesh, states, gate_weight, down_weight)
        R, S, T, C, K = p.R, p.S, p.T, p.C, p.K
        cap, width, fw, hp, pw = p.cap, p.width, p.fw, p.hp, p.pw
        running = halted.reshape(p.rows) == 0
        slot_of = jnp.cumsum(running.astype(jnp.int32)) - 1
        pick = jnp.where(running, slot_of, -1)
        blocks, batch = refill_index.shape
        base = lax.broadcasted_iota(jnp.int32, (blocks, batch), 0) * batch
        fill = jnp.where(running, -1, (base + refill_index).reshape(p.rows))
        bf16, f32 = jnp.bfloat16, jnp.float32
        dma = lambda *shape: pltpu.SemaphoreType.DMA(shape)
        vmem = pl.BlockSpec(memory_space=pltpu.VMEM)
        hbm = pl.BlockSpec(memory_space=pl.ANY)
        return pl.pallas_call(
            functools.partial(block_kernel, p),
            out_shape=jax.ShapeDtypeStruct(states.shape, states.dtype),
            in_specs=[vmem] * 6 + [hbm] * 3,
            out_specs=vmem,
            scratch_shapes=[
                pltpu.VMEM((K, R, cap, width), bf16),
                pltpu.VMEM((p.features, hp), bf16),
                pltpu.VMEM((p.features, hp), bf16),
                pltpu.VMEM((p.halves, p.F, hp, pw), bf16),
                pltpu.VMEM((R, cap, hp), f32),
                pltpu.VMEM((R, cap, hp), f32),
                pltpu.VMEM((R, cap, hp), bf16),
                pltpu.VMEM((cap, width), bf16),
                pltpu.VMEM((C, cap, 128), f32),
                pltpu.VMEM((T, cap, 128), f32),
                pltpu.VMEM((p.parts, T, R, max(1, C - 1), cap, pw), bf16),
                pltpu.VMEM((p.parts, max(1, T - 1), R, cap, pw), bf16),
                pltpu.VMEM((p.parts, R + 1, cap, pw), bf16),
                pltpu.VMEM((p.parts, R, cap, pw), f32),
                dma(p.mats),
                dma(p.mats, R), dma(p.mats, R),
                dma(p.mats, R, S), dma(p.mats, R, S),
                dma(2, R), dma(R),
                dma(R, T), dma(R, T),
                dma(R, T, C), dma(R, T, C),
                dma(C), dma(C), dma(T), dma(T),
                dma(p.parts, T, R, max(1, C - 1)), dma(p.parts, T, R, max(1, C - 1)),
                dma(p.parts, max(1, T - 1), R), dma(p.parts, max(1, T - 1), R),
                dma(p.parts, R), dma(p.parts, R + 1),
                pltpu.SemaphoreType.REGULAR,
            ],
            compiler_params=pltpu.CompilerParams(
                collective_id=0, has_side_effects=True, vmem_limit_bytes=64000 * 1024
            ),
        )(
            pick.reshape(1, p.rows), pick.reshape(p.rows, 1), fill.reshape(p.rows, 1),
            states, fresh_rows, norm_gain.reshape(1, width), gate_weight, up_weight, down_weight,
        )

    return body


def solution(mesh):
    columns = ("tensor", "dp")
    in_specs = (
        P("fsdp", columns),
        P("fsdp", columns),
        P(columns),
        P("fsdp", columns),
        P("fsdp", columns),
        P(columns, "fsdp"),
        P("fsdp", None),
        P("fsdp", None),
    )
    return jax.shard_map(
        make_body(mesh), mesh=mesh, in_specs=in_specs, out_specs=P("fsdp", columns), check_vma=False
    )
```

```python
import functools

import jax
import jax.numpy as jnp
from jax import lax
from jax.experimental import pallas as pl
from jax.experimental.pallas import tpu as pltpu
from jax.sharding import PartitionSpec as P

MESH = pl.DeviceIdType.MESH
norm_eps = 1e-05


class Plan:
    def __init__(self, mesh, states, gate, down):
        self.F, self.T, self.C = (mesh.shape[axis] for axis in ("fsdp", "tensor", "dp"))
        self.R = min(4, max(1, self.F // 2))
        self.S = self.F // self.R
        self.K = self.T * self.C
        self.unit = self.F // self.K
        self.rows, self.width = states.shape
        self.cap = self.rows * 3 // 4
        self.features = self.width * self.K
        self.fw = gate.shape[0]
        self.hp = gate.shape[1] // self.R
        self.halves = self.fw // 128
        self.pw = self.fw // self.halves
        self.mats = 2 + self.halves
        self.parts = self.unit * self.halves


def block_kernel(
    p,
    halted, refill, gain, states_in, fresh_in, gate_w, up_w, down_w,
    result,
    states, fresh, out, picker, spread,
    rows, gate_full, up_full, down_full, gate_acc, up_acc, hidden, kept, ms_c, ms_t,
    crecv, yrecv, zrecv, mine,
    local_sem, gz_send, gz_recv, xs_send, xs_recv, rz_send, rz_recv, ry_send, ry_recv,
    rc_send, rc_recv, mc_send, mc_recv, mt_send, mt_recv,
    oc_send, oc_recv, oy_send, oy_recv, oz_send, oz_recv, pair_sem, in_sem, out_sem,
):
    R, S, T, C, K = p.R, p.S, p.T, p.C, p.K
    cap, width, fw, hp, pw = p.cap, p.width, p.fw, p.hp, p.pw
    f, t, c = lax.axis_index("fsdp"), lax.axis_index("tensor"), lax.axis_index("dp")
    a, b = f // S, f % S
    me = t * C + c

    def remote(src, dst, send_sem, recv_sem, axis, index):
        return pltpu.make_async_remote_copy(
            src_ref=src, dst_ref=dst, send_sem=send_sem, recv_sem=recv_sem,
            device_id={axis: index}, device_id_type=MESH,
        )

    def when(cond, run):
        if cond is True:
            run()
        else:
            pl.when(cond)(run)

    def both(one, two):
        return two if one is True else jnp.logical_and(one, two)

    sent = []

    def send(make, cond=True, log=None):
        when(cond, lambda: make().start())
        (sent if log is None else log).append((make, cond))

    def near(step):
        return [(a - step, a >= step), (a + step, a + step < R)]

    by_distance = [(a, True)] + [pair for step in range(1, R) for pair in near(step)]
    arrivals = by_distance[1:]

    def source_at(m, to):
        if m < 2:
            return (gate_w, up_w)[m].at[:, pl.ds(pl.multiple_of(to * hp, hp), hp)]
        h = m - 2
        return down_w.at[pl.ds(pl.multiple_of(to * hp, hp), hp), h * pw : (h + 1) * pw]

    def full_at(m, owner):
        if m < 2:
            return (gate_full, up_full)[m].at[pl.ds(pl.multiple_of(owner * fw, fw), fw), :]
        return down_full.at[m - 2, owner]

    at_end = jnp.logical_or(a == 0, a == R - 1)

    def send_z(m, steps, where=None, choose=None):
        for step in steps:
            for to, cond in near(step):
                cond = cond if where is None else jnp.logical_and(cond, where)
                cond = cond if choose is None else jnp.logical_and(cond, choose(to))
                send(
                    lambda m=m, to=to: remote(
                        source_at(m, to), full_at(m, f), gz_send.at[m, to], gz_recv.at[m, a],
                        "fsdp", to * S + b,
                    ),
                    cond,
                )

    def wait_z(m, frm):
        place = full_at(m, frm * S + b)
        remote(place, place, gz_send.at[m, frm], gz_recv.at[m, frm], "fsdp", frm * S + b).wait_recv()

    def send_x(m, frm, cond, own=False):
        for step in range(1, S):
            def make(m=m, frm=frm, step=step):
                place = full_at(m, frm * S + b)
                return remote(
                    source_at(m, a) if own else place, place,
                    xs_send.at[m, frm, step], xs_recv.at[m, frm, step],
                    "fsdp", a * S + (b + step) % S,
                )
            send(make, cond)

    def wait_x(m, frm, step):
        owner = (b + S - step) % S
        place = full_at(m, frm * S + owner)
        remote(
            place, place, xs_send.at[m, frm, step], xs_recv.at[m, frm, step], "fsdp", a * S + owner
        ).wait_recv()

    def local(m):
        return pltpu.make_async_copy(source_at(m, a), full_at(m, f), local_sem.at[m])

    def forward_z(m, pairs):
        for frm, cond in pairs:
            when(cond, lambda frm=frm: wait_z(m, frm))
            send_x(m, frm, cond)

    fetch = [
        pltpu.make_async_copy(source, place, in_sem.at[k])
        for k, (source, place) in enumerate(((states_in, states), (fresh_in, fresh)))
    ]
    for copy in fetch:
        copy.start()
    barrier = pltpu.get_barrier_semaphore()
    partners = [("fsdp", ((a + step) % R) * S + b) for step in range(1, R)]
    partners += [("fsdp", a * S + (b + step) % S) for step in range(1, S)]
    partners += [("tensor", (t + step) % T) for step in range(1, T)]
    partners += [("dp", (c + step) % C) for step in range(1, C)]
    for axis, index in partners:
        pl.semaphore_signal(barrier, inc=1, device_id={axis: index}, device_id_type=MESH)
    pl.semaphore_wait(barrier, len(partners))

    far = list(range(2, R))
    close = range(1, min(R, 2))
    send_z(0, close)
    send_x(0, a, True, own=True)
    for m in range(p.mats):
        local(m).start()

    blocks, batch = halted.shape
    f32, bf16, i32 = jnp.float32, jnp.bfloat16, jnp.int32

    def ids(shape, axis):
        return lax.broadcasted_iota(i32, shape, axis)

    within = lax.rem(ids((batch, p.rows), 1), batch) == ids((batch, p.rows), 0)
    block_of = lax.div(ids((blocks, p.rows), 1), batch) == ids((blocks, p.rows), 0)

    def flat(table):
        wide = jnp.dot(table.astype(f32).astype(bf16), within.astype(bf16), preferred_element_type=f32)
        return jnp.sum(jnp.where(block_of, wide, 0.0), axis=0, keepdims=True)

    running = flat((halted[...] == 0).astype(i32))
    upto = (ids((p.rows, p.rows), 0) <= ids((p.rows, p.rows), 1)).astype(bf16)
    count = jnp.dot(jnp.broadcast_to(running, (8, p.rows)).astype(bf16), upto, preferred_element_type=f32)
    slot_row = jnp.where(running > 0.5, count[:1] - 1.0, -1.0).astype(i32)
    picker[...] = (ids((cap, p.rows), 0) == slot_row).astype(bf16)
    fetch[0].wait()
    picked = jnp.dot(picker[...], states[...], preferred_element_type=f32)
    kept[...] = picked.astype(jnp.bfloat16)
    ms_c[c] = jnp.broadcast_to(jnp.sum(picked * picked, axis=-1, keepdims=True), (cap, 128))

    def exchange(buffer, own, axis, count, send_sem, recv_sem):
        def copy(step):
            return remote(
                buffer.at[own], buffer.at[own], send_sem.at[step], recv_sem.at[step],
                axis, (own + step) % count,
            )
        for step in range(1, count):
            send(lambda step=step: copy(step))
        for step in range(1, count):
            place = buffer.at[(own + count - step) % count]
            remote(
                place, place, send_sem.at[step], recv_sem.at[step], axis, (own + count - step) % count
            ).wait_recv()
        return functools.reduce(lambda one, two: one + two, [buffer[k] for k in range(count)])

    ms_t[t] = exchange(ms_c, c, "dp", C, mc_send, mc_recv)
    total_square = exchange(ms_t, t, "tensor", T, mt_send, mt_recv)[:, :1]
    scale = lax.rsqrt(total_square / p.features + norm_eps)
    rows[me, a] = (
        kept[...].astype(jnp.float32) * scale * gain[...].astype(f32).reshape(1, width)
    ).astype(jnp.bfloat16)

    row_sent = []

    def row_z(slot, move, cond):
        way = 0 if move > 0 else 1
        place = lambda: rows.at[me, slot]
        send(
            lambda: remote(
                place(), place(), rz_send.at[way, slot], rz_recv.at[slot], "fsdp", (a + move) * S + b
            ),
            cond, row_sent,
        )

    def row_wait_z(slot):
        place = rows.at[me, slot]
        remote(place, place, rz_send.at[0, slot], rz_recv.at[slot], "fsdp", ((a + 1) % R) * S + b).wait_recv()

    def row_y(slot, cond):
        for step in range(1, T):
            send(
                lambda step=step: remote(
                    rows.at[me, slot], rows.at[me, slot], ry_send.at[slot, step], ry_recv.at[slot, step],
                    "tensor", (t + step) % T,
                ),
                cond, row_sent,
            )

    def row_c(slot, tstep, cond):
        block = ((t + T - tstep) % T) * C + c
        for step in range(1, C):
            send(
                lambda step=step: remote(
                    rows.at[block, slot], rows.at[block, slot],
                    rc_send.at[slot, tstep, step], rc_recv.at[slot, tstep, step],
                    "dp", (c + step) % C,
                ),
                cond, row_sent,
            )

    def row_step(step):
        for (slot, cond), move in zip(near(step), (1, -1)):
            when(cond, lambda slot=slot: row_wait_z(slot))
            more = (a + 1 < R) if move > 0 else (a > 0)
            row_z(slot, move, both(cond, more))
            row_y(slot, cond)
            row_c(slot, 0, cond)

    row_z(a, 1, a + 1 < R)
    row_z(a, -1, a > 0)
    send_z(1, close, at_end)
    row_y(a, True)
    row_c(a, 0, True)
    for m in range(1, p.mats):
        send_x(m, a, True, own=True)

    base = lax.div(ids((1, p.rows), 1), batch) * batch
    fresh_row = jnp.where(running > 0.5, -1, flat(refill[...]).astype(i32) + base)
    filler = (ids((p.rows, p.rows), 0) == fresh_row).astype(bf16)
    turned = (((0,), (0,)), ((), ()))
    fetch[1].wait()
    out[...] = lax.dot_general(filler, fresh[...], turned, preferred_element_type=f32).astype(bf16)
    same = (ids((cap, cap), 0) == ids((cap, cap), 1)).astype(bf16)
    spread[...] = lax.dot_general(picker[...], same, turned, preferred_element_type=f32).astype(bf16)

    def row_arrive_y(pairs):
        for slot, cond in pairs:
            for tstep in range(1, T):
                place = lambda: rows.at[((t + T - tstep) % T) * C + c, slot]
                when(
                    cond,
                    lambda: remote(
                        place(), place(), ry_send.at[slot, tstep], ry_recv.at[slot, tstep],
                        "tensor", (t + T - tstep) % T,
                    ).wait_recv(),
                )
                row_c(slot, tstep, cond)

    inner = jnp.logical_not(at_end)
    beyond = range(3, R)

    def only(pairs, where):
        return [(frm, both(cond, where)) for frm, cond in pairs]

    def rim(pairs, yes):
        picked = []
        for frm, cond in pairs:
            end = jnp.logical_or(frm == 0, frm == R - 1)
            picked.append((frm, both(cond, end if yes else jnp.logical_not(end))))
        return picked

    for step in range(1, min(R, 3)):
        row_step(step)
        if step == 1:
            forward_z(0, near(1))
    send_z(1, close, inner, lambda to: jnp.logical_and(to > 0, to < R - 1))
    send_z(0, far, inner)
    send_z(1, far, inner)
    forward_z(0, only(near(2), at_end))
    forward_z(1, only(near(2), at_end))
    if C > 1:
        @pl.when(at_end)
        def _():
            for step in range(1, C):
                pl.semaphore_signal(
                    pair_sem, inc=1, device_id={"dp": (c + step) % C}, device_id_type=MESH
                )
            pl.semaphore_wait(pair_sem, C - 1)

    for m in range(2):
        send_z(m, far[:1], at_end)
    for step in beyond:
        row_step(step)
    for m in range(2):
        send_z(m, beyond, at_end)
    for h in range(p.halves):
        send_z(2 + h, close, at_end)
    send_z(2, far, at_end)
    row_arrive_y(by_distance[:3])
    forward_z(1, only(near(1), inner))
    row_arrive_y(by_distance[3:])
    send_z(1, close, inner, lambda to: jnp.logical_or(to == 0, to == R - 1))
    forward_z(1, only(near(1), at_end))
    forward_z(0, only(near(2), inner))
    for slot in range(R):
        for tstep in range(T):
            for step in range(1, C):
                place = rows.at[((t + T - tstep) % T) * C + (c + C - step) % C, slot]
                remote(
                    place, place, rc_send.at[slot, tstep, step], rc_recv.at[slot, tstep, step],
                    "dp", (c + C - step) % C,
                ).wait_recv()
    for h in range(p.halves):
        send_z(2 + h, close, inner)
        send_z(2 + h, far, inner)

    per_owner = S // p.unit
    for m in range(p.mats):
        local(m).wait()

    def product_block(block, weights, acc, first):
        span = pl.ds(pl.multiple_of(block * width, width), width)

        def body(slot, carry):
            part = jnp.dot(rows[block, slot], weights[span, :], preferred_element_type=jnp.float32)
            acc[slot] = part if first else acc[slot] + part
            return carry

        lax.fori_loop(0, R, body, 0)

    def products(m, pairs):
        weights, acc = ((gate_full, gate_acc), (up_full, up_acc))[m]
        for frm, cond in pairs:
            def run(frm=frm, first=cond is True):
                for step in range(1, S):
                    wait_x(m, frm, step)
                for k in range(per_owner):
                    product_block(frm * per_owner + k, weights, acc, first and k == 0)
            when(cond, run)

    products(0, by_distance[:1])
    products(0, near(1))
    forward_z(1, only(near(2), inner))
    products(0, only(near(2), at_end))
    for step in beyond:
        forward_z(0, near(step))
    products(1, by_distance[:1])
    products(1, only(near(2), at_end))
    products(1, near(1))
    for step in beyond:
        forward_z(1, near(step))
        products(0, near(step))
    products(0, only(near(2), inner))
    products(1, only(near(2), inner))
    for step in beyond:
        products(1, near(step))

    def activate(slot, carry):
        gate = gate_acc[slot]
        hidden[slot] = (gate / (1.0 + jnp.exp(-gate)) * up_acc[slot]).astype(jnp.bfloat16)
        return carry

    lax.fori_loop(0, R, activate, 0)
    for make, cond in row_sent:
        when(cond, lambda make=make: make().wait_send())

    def slot_at(index):
        return jnp.where(index % 2 == 0, R - 1 - index // 2, index // 2)

    def column_part(n):
        return n // p.unit, (b + n % p.unit) % p.unit

    def product(n, slot, block):
        h, i = column_part(n)
        return jnp.dot(hidden[slot], down_full[h, block * p.unit + i], preferred_element_type=jnp.float32)

    def stage(n, block, slot):
        return rows.at[block, slot, :, n * pw : (n + 1) * pw]

    def out_c(n, tstep, slot, step):
        return remote(
            stage(n, tstep * (C - 1) + step - 1, slot), crecv.at[n, tstep, slot, step - 1],
            oc_send.at[n, tstep, slot, step - 1], oc_recv.at[n, tstep, slot, step - 1],
            "dp", (c + step) % C,
        )

    def out_y(n, tstep, slot):
        return remote(
            stage(n, T * (C - 1) + tstep, slot), yrecv.at[n, tstep, slot],
            oy_send.at[n, tstep, slot], oy_recv.at[n, tstep, slot],
            "tensor", (t + 1 + tstep) % T,
        )

    def out_z(n, slot):
        to = jnp.where(slot > a, a + 1, a - 1)
        land = jnp.where(slot == a - 1, R, slot)
        return remote(
            stage(n, K - 1, slot), zrecv.at[n, land], oz_send.at[n, slot], oz_recv.at[n, land],
            "fsdp", to * S + b,
        )

    def wait_out_z(n, land):
        place = zrecv.at[n, land]
        remote(place, place, oz_send.at[n, 0], oz_recv.at[n, land], "fsdp", ((a + 1) % R) * S + b).wait_recv()

    def part_a(n):
        h, turn = n // p.unit, n % p.unit
        m = 2 + h
        if turn == 0:
            forward_z(m, arrivals)
            if h + 1 < p.halves:
                send_z(m + 1, far, at_end)
        for frm in range(R):
            for step in range(1, S):
                if (step + turn) % p.unit == 0:
                    wait_x(m, frm, step)

        def body(index, carry):
            tstep, slot = index // R, slot_at(index % R)
            for step in range(1, C):
                block = ((t + 1 + tstep) % T) * C + (c + step) % C
                place = stage(n, tstep * (C - 1) + step - 1, slot)
                place[...] = product(n, slot, block).astype(jnp.bfloat16)
                out_c(n, tstep, slot, step).start()
            return carry

        lax.fori_loop(0, T * R, body, 0)

    def chip_sum(n, tstep, slot):
        value = product(n, slot, ((t + 1 + tstep) % T) * C + c)
        for step in range(1, C):
            out_c(n, tstep, slot, step).wait_recv()
            value = value + crecv[n, tstep, slot, step - 1].astype(jnp.float32)
        return value

    def part_b(n, low, high):
        def body(index, carry):
            tstep, slot = index // (high - low), slot_at(low + index % (high - low))
            place = stage(n, T * (C - 1) + tstep, slot)
            place[...] = chip_sum(n, tstep, slot).astype(jnp.bfloat16)
            out_y(n, tstep, slot).start()
            return carry

        if high > low:
            lax.fori_loop(0, (T - 1) * (high - low), body, 0)

    def pass_on(n, slot, value):
        place = stage(n, K - 1, slot)
        place[...] = value.astype(jnp.bfloat16)
        out_z(n, slot).start()

    def part_c(n, low, high):
        def body(index, carry):
            slot = slot_at(index)
            value = chip_sum(n, T - 1, slot)
            for tstep in range(T - 1):
                out_y(n, tstep, slot).wait_recv()
                value = value + yrecv[n, tstep, slot].astype(jnp.float32)
            mine[n, slot] = value
            head = jnp.logical_or(
                jnp.logical_and(a == 0, slot > a), jnp.logical_and(a == R - 1, slot < a)
            )
            pl.when(head)(lambda: pass_on(n, slot, mine[n, slot]))
            return carry

        lax.fori_loop(low, high, body, 0)

    def part_s(n, low, high, hop):
        def body(index, carry):
            slot = slot_at(index)
            up = jnp.logical_and(a == hop, slot > a)
            down = jnp.logical_and(a == R - 1 - hop, slot < a)

            @pl.when(jnp.logical_or(up, down))
            def _():
                wait_out_z(n, slot)
                pass_on(n, slot, mine[n, slot] + zrecv[n, slot].astype(jnp.float32))

            return carry

        lax.fori_loop(low, high, body, 0)

    def part_f(n):
        for cond, land in ((a > 0, a), (a < R - 1, R)):
            @pl.when(cond)
            def _():
                wait_out_z(n, land)
                mine[n, a] = mine[n, a] + zrecv[n, land].astype(jnp.float32)

        h, i = column_part(n)
        columns = pl.ds(pl.multiple_of(i * fw + h * pw, pw), pw)
        settled = (kept[:, columns].astype(jnp.float32) + mine[n, a]).astype(jnp.bfloat16)
        placed = jnp.dot(spread[...], settled, preferred_element_type=jnp.float32)
        out[:, columns] = (placed + out[:, columns].astype(jnp.float32)).astype(jnp.bfloat16)
        write_out(n).start()

    def write_out(n):
        h, i = column_part(n)
        columns = pl.ds(pl.multiple_of(i * fw + h * pw, pw), pw)
        return pltpu.make_async_copy(out.at[:, columns], result.at[:, columns], out_sem.at[n])

    behind = 2
    for tick in range(p.parts + behind + R - 1):
        if tick < p.parts:
            part_a(tick)
            part_b(tick, 0, R)
        if 0 <= tick - behind < p.parts:
            part_c(tick - behind, 0, R)
        for hop in range(1, R - 1):
            if 0 <= tick - behind + 1 - hop < p.parts:
                part_s(tick - behind + 1 - hop, 0, R, hop)
        if 0 <= tick - behind - R + 2 < p.parts:
            part_f(tick - behind - R + 2)

    for make, cond in sent:
        when(cond, lambda make=make: make().wait_send())

    def settle(index, carry):
        n, slot = index // R, index % R
        for tstep in range(T):
            for step in range(1, C):
                place = crecv.at[n, tstep, slot, step - 1]
                remote(
                    place, place, oc_send.at[n, tstep, slot, step - 1],
                    oc_recv.at[n, tstep, slot, step - 1], "dp", (c + step) % C,
                ).wait_send()
        for tstep in range(T - 1):
            place = yrecv.at[n, tstep, slot]
            remote(
                place, place, oy_send.at[n, tstep, slot], oy_recv.at[n, tstep, slot],
                "tensor", (t + 1 + tstep) % T,
            ).wait_send()

        @pl.when(slot != a)
        def _():
            place = zrecv.at[n, slot]
            remote(
                place, place, oz_send.at[n, slot], oz_recv.at[n, slot],
                "fsdp", ((a + 1) % R) * S + b,
            ).wait_send()

        return carry

    lax.fori_loop(0, p.parts * R, settle, 0)
    for n in range(p.parts):
        write_out(n).wait()


def make_body(mesh):
    def body(states, fresh_rows, norm_gain, gate_weight, up_weight, down_weight, halted, refill_index):
        p = Plan(mesh, states, gate_weight, down_weight)
        R, S, T, C, K = p.R, p.S, p.T, p.C, p.K
        cap, width, fw, hp, pw = p.cap, p.width, p.fw, p.hp, p.pw
        bf16, f32 = jnp.bfloat16, jnp.float32
        dma = lambda *shape: pltpu.SemaphoreType.DMA(shape)
        vmem = pl.BlockSpec(memory_space=pltpu.VMEM)
        hbm = pl.BlockSpec(memory_space=pl.ANY)
        return pl.pallas_call(
            functools.partial(block_kernel, p),
            out_shape=jax.ShapeDtypeStruct(states.shape, states.dtype),
            in_specs=[vmem] * 3 + [hbm] * 5,
            out_specs=hbm,
            scratch_shapes=[
                pltpu.VMEM((p.rows, width), bf16),
                pltpu.VMEM((p.rows, width), bf16),
                pltpu.VMEM((p.rows, width), bf16),
                pltpu.VMEM((cap, p.rows), bf16),
                pltpu.VMEM((p.rows, cap), bf16),
                pltpu.VMEM((K, R, cap, width), bf16),
                pltpu.VMEM((p.features, hp), bf16),
                pltpu.VMEM((p.features, hp), bf16),
                pltpu.VMEM((p.halves, p.F, hp, pw), bf16),
                pltpu.VMEM((R, cap, hp), f32),
                pltpu.VMEM((R, cap, hp), f32),
                pltpu.VMEM((R, cap, hp), bf16),
                pltpu.VMEM((cap, width), bf16),
                pltpu.VMEM((C, cap, 128), f32),
                pltpu.VMEM((T, cap, 128), f32),
                pltpu.VMEM((p.parts, T, R, max(1, C - 1), cap, pw), bf16),
                pltpu.VMEM((p.parts, max(1, T - 1), R, cap, pw), bf16),
                pltpu.VMEM((p.parts, R + 1, cap, pw), bf16),
                pltpu.VMEM((p.parts, R, cap, pw), f32),
                dma(p.mats),
                dma(p.mats, R), dma(p.mats, R),
                dma(p.mats, R, S), dma(p.mats, R, S),
                dma(2, R), dma(R),
                dma(R, T), dma(R, T),
                dma(R, T, C), dma(R, T, C),
                dma(C), dma(C), dma(T), dma(T),
                dma(p.parts, T, R, max(1, C - 1)), dma(p.parts, T, R, max(1, C - 1)),
                dma(p.parts, max(1, T - 1), R), dma(p.parts, max(1, T - 1), R),
                dma(p.parts, R), dma(p.parts, R + 1),
                pltpu.SemaphoreType.REGULAR,
                dma(2), dma(p.parts),
            ],
            compiler_params=pltpu.CompilerParams(
                collective_id=0, has_side_effects=True, vmem_limit_bytes=64000 * 1024
            ),
        )(
            halted, refill_index, norm_gain, states, fresh_rows, gate_weight, up_weight, down_weight,
        )

    return body


def solution(mesh):
    columns = ("tensor", "dp")
    in_specs = (
        P("fsdp", columns),
        P("fsdp", columns),
        P(columns),
        P("fsdp", columns),
        P("fsdp", columns),
        P(columns, "fsdp"),
        P("fsdp", None),
        P("fsdp", None),
    )
    return jax.shard_map(
        make_body(mesh), mesh=mesh, in_specs=in_specs, out_specs=P("fsdp", columns), check_vma=False
    )
```

```python
import functools

import jax
import jax.numpy as jnp
from jax import lax
from jax.experimental import pallas as pl
from jax.experimental.pallas import tpu as pltpu
from jax.sharding import PartitionSpec as P

MESH = pl.DeviceIdType.MESH
norm_eps = 1e-05


class Plan:
    def __init__(self, mesh, states, gate, down):
        self.F, self.T, self.C = (mesh.shape[axis] for axis in ("fsdp", "tensor", "dp"))
        self.R = min(4, max(1, self.F // 2))
        self.S = self.F // self.R
        self.K = self.T * self.C
        self.unit = self.F // self.K
        self.rows, self.width = states.shape
        self.cap = self.rows * 3 // 4
        self.features = self.width * self.K
        self.fw = gate.shape[0]
        self.hp = gate.shape[1] // self.R
        self.halves = self.fw // 128
        self.pw = self.fw // self.halves
        self.gates, self.ups = [0, 1], [2, 3]
        self.down0 = 4
        self.mats = self.down0 + self.halves
        self.parts = self.unit * self.halves


def block_kernel(
    p,
    halted, refill, gain, states_in, fresh_in, gate_w, up_w, down_w,
    result,
    states, fresh, out, picker, spread,
    rows, gate_full, up_full, down_full, gate_acc, up_acc, hidden, kept, ms_c, ms_t,
    crecv, yrecv, zrecv, mine,
    local_sem, gz_send, gz_recv, xs_send, xs_recv, rz_send, rz_recv, ry_send, ry_recv,
    rc_send, rc_recv, mc_send, mc_recv, mt_send, mt_recv,
    oc_send, oc_recv, oy_send, oy_recv, oz_send, oz_recv, pair_sem, in_sem, out_sem,
):
    R, S, T, C, K = p.R, p.S, p.T, p.C, p.K
    cap, width, fw, hp, pw = p.cap, p.width, p.fw, p.hp, p.pw
    f, t, c = lax.axis_index("fsdp"), lax.axis_index("tensor"), lax.axis_index("dp")
    a, b = f // S, f % S
    me = t * C + c

    def remote(src, dst, send_sem, recv_sem, axis, index):
        return pltpu.make_async_remote_copy(
            src_ref=src, dst_ref=dst, send_sem=send_sem, recv_sem=recv_sem,
            device_id={axis: index}, device_id_type=MESH,
        )

    def when(cond, run):
        if cond is True:
            run()
        else:
            pl.when(cond)(run)

    def both(one, two):
        return two if one is True else jnp.logical_and(one, two)

    sent = []

    def send(make, cond=True, log=None):
        when(cond, lambda: make().start())
        (sent if log is None else log).append((make, cond))

    def near(step):
        return [(a - step, a >= step), (a + step, a + step < R)]

    by_distance = [(a, True)] + [pair for step in range(1, R) for pair in near(step)]
    arrivals = by_distance[1:]

    gates, ups, down0 = p.gates, p.ups, p.down0
    sub = fw // len(ups)

    def source_at(m, to):
        columns = pl.ds(pl.multiple_of(to * hp, hp), hp)
        if m < down0:
            k = m % len(ups)
            return (gate_w if m in gates else up_w).at[k * sub : (k + 1) * sub, columns]
        h = m - down0
        return down_w.at[columns, h * pw : (h + 1) * pw]

    def full_at(m, owner):
        if m < down0:
            span = pl.ds(pl.multiple_of(owner * fw + (m % len(ups)) * sub, sub), sub)
            return (gate_full if m in gates else up_full).at[span, :]
        return down_full.at[m - down0, owner]

    at_end = jnp.logical_or(a == 0, a == R - 1)

    def send_z(m, steps, where=None, choose=None):
        for step in steps:
            for to, cond in near(step):
                cond = cond if where is None else jnp.logical_and(cond, where)
                cond = cond if choose is None else jnp.logical_and(cond, choose(to))
                send(
                    lambda m=m, to=to: remote(
                        source_at(m, to), full_at(m, f), gz_send.at[m, to], gz_recv.at[m, a],
                        "fsdp", to * S + b,
                    ),
                    cond,
                )

    def wait_z(m, frm):
        place = full_at(m, frm * S + b)
        remote(place, place, gz_send.at[m, frm], gz_recv.at[m, frm], "fsdp", frm * S + b).wait_recv()

    def send_x(m, frm, cond, own=False):
        for step in range(1, S):
            def make(m=m, frm=frm, step=step):
                place = full_at(m, frm * S + b)
                return remote(
                    source_at(m, a) if own else place, place,
                    xs_send.at[m, frm, step], xs_recv.at[m, frm, step],
                    "fsdp", a * S + (b + step) % S,
                )
            send(make, cond)

    def wait_x(m, frm, step):
        owner = (b + S - step) % S
        place = full_at(m, frm * S + owner)
        remote(
            place, place, xs_send.at[m, frm, step], xs_recv.at[m, frm, step], "fsdp", a * S + owner
        ).wait_recv()

    def local(m):
        return pltpu.make_async_copy(source_at(m, a), full_at(m, f), local_sem.at[m])

    def forward_z(m, pairs):
        for frm, cond in pairs:
            when(cond, lambda frm=frm: wait_z(m, frm))
            send_x(m, frm, cond)

    fetch = [
        pltpu.make_async_copy(source, place, in_sem.at[k])
        for k, (source, place) in enumerate(((states_in, states), (fresh_in, fresh)))
    ]
    for copy in fetch:
        copy.start()
    barrier = pltpu.get_barrier_semaphore()
    partners = [("fsdp", ((a + step) % R) * S + b) for step in range(1, R)]
    partners += [("fsdp", a * S + (b + step) % S) for step in range(1, S)]
    partners += [("tensor", (t + step) % T) for step in range(1, T)]
    partners += [("dp", (c + step) % C) for step in range(1, C)]
    for axis, index in partners:
        pl.semaphore_signal(barrier, inc=1, device_id={axis: index}, device_id_type=MESH)
    pl.semaphore_wait(barrier, len(partners))

    far = list(range(2, R))
    close = range(1, min(R, 2))
    for m in gates:
        send_z(m, close)
    for m in gates:
        send_x(m, a, True, own=True)
    for m in range(p.mats):
        local(m).start()

    blocks, batch = halted.shape
    f32, bf16, i32 = jnp.float32, jnp.bfloat16, jnp.int32

    def ids(shape, axis):
        return lax.broadcasted_iota(i32, shape, axis)

    within = lax.rem(ids((batch, p.rows), 1), batch) == ids((batch, p.rows), 0)
    block_of = lax.div(ids((blocks, p.rows), 1), batch) == ids((blocks, p.rows), 0)

    def flat(table):
        wide = jnp.dot(table.astype(f32).astype(bf16), within.astype(bf16), preferred_element_type=f32)
        return jnp.sum(jnp.where(block_of, wide, 0.0), axis=0, keepdims=True)

    running = flat((halted[...] == 0).astype(i32))
    upto = (ids((p.rows, p.rows), 0) <= ids((p.rows, p.rows), 1)).astype(bf16)
    count = jnp.dot(jnp.broadcast_to(running, (8, p.rows)).astype(bf16), upto, preferred_element_type=f32)
    slot_row = jnp.where(running > 0.5, count[:1] - 1.0, -1.0).astype(i32)
    picker[...] = (ids((cap, p.rows), 0) == slot_row).astype(bf16)
    fetch[0].wait()
    picked = jnp.dot(picker[...], states[...], preferred_element_type=f32)
    kept[...] = picked.astype(jnp.bfloat16)
    ms_c[c] = jnp.broadcast_to(jnp.sum(picked * picked, axis=-1, keepdims=True), (cap, 128))

    def exchange(buffer, own, axis, count, send_sem, recv_sem):
        def copy(step):
            return remote(
                buffer.at[own], buffer.at[own], send_sem.at[step], recv_sem.at[step],
                axis, (own + step) % count,
            )
        for step in range(1, count):
            send(lambda step=step: copy(step))
        for step in range(1, count):
            place = buffer.at[(own + count - step) % count]
            remote(
                place, place, send_sem.at[step], recv_sem.at[step], axis, (own + count - step) % count
            ).wait_recv()
        return functools.reduce(lambda one, two: one + two, [buffer[k] for k in range(count)])

    ms_t[t] = exchange(ms_c, c, "dp", C, mc_send, mc_recv)
    total_square = exchange(ms_t, t, "tensor", T, mt_send, mt_recv)[:, :1]
    scale = lax.rsqrt(total_square / p.features + norm_eps)
    rows[me, a] = (
        kept[...].astype(jnp.float32) * scale * gain[...].astype(f32).reshape(1, width)
    ).astype(jnp.bfloat16)

    row_sent = []

    def row_z(slot, move, cond):
        way = 0 if move > 0 else 1
        place = lambda: rows.at[me, slot]
        send(
            lambda: remote(
                place(), place(), rz_send.at[way, slot], rz_recv.at[slot], "fsdp", (a + move) * S + b
            ),
            cond, row_sent,
        )

    def row_wait_z(slot):
        place = rows.at[me, slot]
        remote(place, place, rz_send.at[0, slot], rz_recv.at[slot], "fsdp", ((a + 1) % R) * S + b).wait_recv()

    def row_y(slot, cond):
        for step in range(1, T):
            send(
                lambda step=step: remote(
                    rows.at[me, slot], rows.at[me, slot], ry_send.at[slot, step], ry_recv.at[slot, step],
                    "tensor", (t + step) % T,
                ),
                cond, row_sent,
            )

    def row_c(slot, tstep, cond):
        block = ((t + T - tstep) % T) * C + c
        for step in range(1, C):
            send(
                lambda step=step: remote(
                    rows.at[block, slot], rows.at[block, slot],
                    rc_send.at[slot, tstep, step], rc_recv.at[slot, tstep, step],
                    "dp", (c + step) % C,
                ),
                cond, row_sent,
            )

    def row_step(step):
        for (slot, cond), move in zip(near(step), (1, -1)):
            when(cond, lambda slot=slot: row_wait_z(slot))
            more = (a + 1 < R) if move > 0 else (a > 0)
            row_z(slot, move, both(cond, more))
            row_y(slot, cond)
            row_c(slot, 0, cond)

    row_z(a, 1, a + 1 < R)
    row_z(a, -1, a > 0)
    for m in ups:
        send_z(m, close, at_end)
    row_y(a, True)
    row_c(a, 0, True)
    for m in range(len(gates), p.mats):
        send_x(m, a, True, own=True)

    base = lax.div(ids((1, p.rows), 1), batch) * batch
    fresh_row = jnp.where(running > 0.5, -1, flat(refill[...]).astype(i32) + base)
    filler = (ids((p.rows, p.rows), 0) == fresh_row).astype(bf16)
    turned = (((0,), (0,)), ((), ()))
    fetch[1].wait()
    out[...] = lax.dot_general(filler, fresh[...], turned, preferred_element_type=f32).astype(bf16)
    same = (ids((cap, cap), 0) == ids((cap, cap), 1)).astype(bf16)
    spread[...] = lax.dot_general(picker[...], same, turned, preferred_element_type=f32).astype(bf16)

    def row_arrive_y(pairs):
        for slot, cond in pairs:
            for tstep in range(1, T):
                place = lambda: rows.at[((t + T - tstep) % T) * C + c, slot]
                when(
                    cond,
                    lambda: remote(
                        place(), place(), ry_send.at[slot, tstep], ry_recv.at[slot, tstep],
                        "tensor", (t + T - tstep) % T,
                    ).wait_recv(),
                )
                row_c(slot, tstep, cond)

    inner = jnp.logical_not(at_end)
    beyond = range(3, R)

    def only(pairs, where):
        return [(frm, both(cond, where)) for frm, cond in pairs]

    def rim(pairs, yes):
        picked = []
        for frm, cond in pairs:
            end = jnp.logical_or(frm == 0, frm == R - 1)
            picked.append((frm, both(cond, end if yes else jnp.logical_not(end))))
        return picked

    for step in range(1, min(R, 3)):
        row_step(step)
        if step == 1:
            for m in gates:
                forward_z(m, near(1))
    for m in ups:
        send_z(m, close, inner, lambda to: jnp.logical_and(to > 0, to < R - 1))
    for m in gates:
        send_z(m, far, inner)
    for m in ups:
        send_z(m, far, inner)
    for m in gates:
        forward_z(m, only(near(2), at_end))
    for m in ups:
        forward_z(m, only(near(2), at_end))
    if C > 1:
        @pl.when(at_end)
        def _():
            for step in range(1, C):
                pl.semaphore_signal(
                    pair_sem, inc=1, device_id={"dp": (c + step) % C}, device_id_type=MESH
                )
            pl.semaphore_wait(pair_sem, C - 1)

    for m in (*gates, *ups):
        send_z(m, far[:1], at_end)
    for step in beyond:
        row_step(step)
    for m in (*gates, *ups):
        send_z(m, beyond, at_end)
    send_z(down0, close, at_end)
    send_z(down0, far, at_end)
    for h in range(1, p.halves):
        send_z(down0 + h, close, at_end)
    row_arrive_y(by_distance[:3])
    for m in ups:
        forward_z(m, only(near(1), inner))
    row_arrive_y(by_distance[3:])
    for m in ups:
        send_z(m, close, inner, lambda to: jnp.logical_or(to == 0, to == R - 1))
    for m in ups:
        forward_z(m, only(near(1), at_end))
    for m in gates:
        forward_z(m, only(near(2), inner))
    for slot in range(R):
        for tstep in range(T):
            for step in range(1, C):
                place = rows.at[((t + T - tstep) % T) * C + (c + C - step) % C, slot]
                remote(
                    place, place, rc_send.at[slot, tstep, step], rc_recv.at[slot, tstep, step],
                    "dp", (c + C - step) % C,
                ).wait_recv()
    for h in range(p.halves):
        send_z(down0 + h, close, inner)
        send_z(down0 + h, far, inner)

    per_owner = S // p.unit
    for m in range(p.mats):
        local(m).wait()

    def product_block(block, weights, acc, first):
        span = pl.ds(pl.multiple_of(block * width, width), width)

        def body(slot, carry):
            part = jnp.dot(rows[block, slot], weights[span, :], preferred_element_type=jnp.float32)
            acc[slot] = part if first else acc[slot] + part
            return carry

        lax.fori_loop(0, R, body, 0)

    def products(m, pairs):
        weights, acc = ((gate_full, gate_acc), (up_full, up_acc))[m]
        for frm, cond in pairs:
            def run(frm=frm, first=cond is True):
                for step in range(1, S):
                    for piece in ups if m else gates:
                        wait_x(piece, frm, step)
                for k in range(per_owner):
                    product_block(frm * per_owner + k, weights, acc, first and k == 0)
            when(cond, run)

    products(0, by_distance[:1])
    products(0, near(1))
    for m in ups:
        forward_z(m, only(near(2), inner))
    products(0, only(near(2), at_end))
    for step in beyond:
        for m in gates:
            forward_z(m, near(step))
    products(1, by_distance[:1])
    products(1, only(near(2), at_end))
    products(1, near(1))
    for step in beyond:
        for m in ups:
            forward_z(m, near(step))
        products(0, near(step))
    products(0, only(near(2), inner))
    products(1, only(near(2), inner))
    for step in beyond:
        products(1, near(step))

    def activate(slot, carry):
        gate = gate_acc[slot]
        hidden[slot] = (gate / (1.0 + jnp.exp(-gate)) * up_acc[slot]).astype(jnp.bfloat16)
        return carry

    lax.fori_loop(0, R, activate, 0)
    for make, cond in row_sent:
        when(cond, lambda make=make: make().wait_send())

    def slot_at(index):
        return jnp.where(index % 2 == 0, R - 1 - index // 2, index // 2)

    def column_part(n):
        return n // p.unit, (b + n % p.unit) % p.unit

    def product(n, slot, block):
        h, i = column_part(n)
        return jnp.dot(hidden[slot], down_full[h, block * p.unit + i], preferred_element_type=jnp.float32)

    def stage(n, block, slot):
        return rows.at[block, slot, :, n * pw : (n + 1) * pw]

    def out_c(n, tstep, slot, step):
        return remote(
            stage(n, tstep * (C - 1) + step - 1, slot), crecv.at[n, tstep, slot, step - 1],
            oc_send.at[n, tstep, slot, step - 1], oc_recv.at[n, tstep, slot, step - 1],
            "dp", (c + step) % C,
        )

    def out_y(n, tstep, slot):
        return remote(
            stage(n, T * (C - 1) + tstep, slot), yrecv.at[n, tstep, slot],
            oy_send.at[n, tstep, slot], oy_recv.at[n, tstep, slot],
            "tensor", (t + 1 + tstep) % T,
        )

    def out_z(n, slot):
        to = jnp.where(slot > a, a + 1, a - 1)
        land = jnp.where(slot == a - 1, R, slot)
        return remote(
            stage(n, K - 1, slot), zrecv.at[n, land], oz_send.at[n, slot], oz_recv.at[n, land],
            "fsdp", to * S + b,
        )

    def wait_out_z(n, land):
        place = zrecv.at[n, land]
        remote(place, place, oz_send.at[n, 0], oz_recv.at[n, land], "fsdp", ((a + 1) % R) * S + b).wait_recv()

    def part_a(n):
        h, turn = n // p.unit, n % p.unit
        m = down0 + h
        if turn == 0:
            forward_z(m, arrivals)
            if h + 1 < p.halves:
                send_z(m + 1, far, at_end)
        for frm in range(R):
            for step in range(1, S):
                if (step + turn) % p.unit == 0:
                    wait_x(m, frm, step)

        def body(index, carry):
            tstep, slot = index // R, slot_at(index % R)
            for step in range(1, C):
                block = ((t + 1 + tstep) % T) * C + (c + step) % C
                place = stage(n, tstep * (C - 1) + step - 1, slot)
                place[...] = product(n, slot, block).astype(jnp.bfloat16)
                out_c(n, tstep, slot, step).start()
            return carry

        lax.fori_loop(0, T * R, body, 0)

    def chip_sum(n, tstep, slot):
        value = product(n, slot, ((t + 1 + tstep) % T) * C + c)
        for step in range(1, C):
            out_c(n, tstep, slot, step).wait_recv()
            value = value + crecv[n, tstep, slot, step - 1].astype(jnp.float32)
        return value

    def part_b(n, low, high):
        def body(index, carry):
            tstep, slot = index // (high - low), slot_at(low + index % (high - low))
            place = stage(n, T * (C - 1) + tstep, slot)
            place[...] = chip_sum(n, tstep, slot).astype(jnp.bfloat16)
            out_y(n, tstep, slot).start()
            return carry

        if high > low:
            lax.fori_loop(0, (T - 1) * (high - low), body, 0)

    def pass_on(n, slot, value):
        place = stage(n, K - 1, slot)
        place[...] = value.astype(jnp.bfloat16)
        out_z(n, slot).start()

    def part_c(n, low, high):
        def body(index, carry):
            slot = slot_at(index)
            value = chip_sum(n, T - 1, slot)
            for tstep in range(T - 1):
                out_y(n, tstep, slot).wait_recv()
                value = value + yrecv[n, tstep, slot].astype(jnp.float32)
            mine[n, slot] = value
            head = jnp.logical_or(
                jnp.logical_and(a == 0, slot > a), jnp.logical_and(a == R - 1, slot < a)
            )
            pl.when(head)(lambda: pass_on(n, slot, mine[n, slot]))
            return carry

        lax.fori_loop(low, high, body, 0)

    def part_s(n, low, high, hop):
        def body(index, carry):
            slot = slot_at(index)
            up = jnp.logical_and(a == hop, slot > a)
            down = jnp.logical_and(a == R - 1 - hop, slot < a)

            @pl.when(jnp.logical_or(up, down))
            def _():
                wait_out_z(n, slot)
                pass_on(n, slot, mine[n, slot] + zrecv[n, slot].astype(jnp.float32))

            return carry

        lax.fori_loop(low, high, body, 0)

    def part_f(n):
        for cond, land in ((a > 0, a), (a < R - 1, R)):
            @pl.when(cond)
            def _():
                wait_out_z(n, land)
                mine[n, a] = mine[n, a] + zrecv[n, land].astype(jnp.float32)

        h, i = column_part(n)
        columns = pl.ds(pl.multiple_of(i * fw + h * pw, pw), pw)
        settled = (kept[:, columns].astype(jnp.float32) + mine[n, a]).astype(jnp.bfloat16)
        placed = jnp.dot(spread[...], settled, preferred_element_type=jnp.float32)
        out[:, columns] = (placed + out[:, columns].astype(jnp.float32)).astype(jnp.bfloat16)
        write_out(n).start()

    def write_out(n):
        h, i = column_part(n)
        columns = pl.ds(pl.multiple_of(i * fw + h * pw, pw), pw)
        return pltpu.make_async_copy(out.at[:, columns], result.at[:, columns], out_sem.at[n])

    behind = 2
    for tick in range(p.parts + behind + R - 1):
        if tick < p.parts:
            part_a(tick)
            part_b(tick, 0, R)
        if 0 <= tick - behind < p.parts:
            part_c(tick - behind, 0, R)
        for hop in range(1, R - 1):
            if 0 <= tick - behind + 1 - hop < p.parts:
                part_s(tick - behind + 1 - hop, 0, R, hop)
        if 0 <= tick - behind - R + 2 < p.parts:
            part_f(tick - behind - R + 2)

    for make, cond in sent:
        when(cond, lambda make=make: make().wait_send())

    def settle(index, carry):
        n, slot = index // R, index % R
        for tstep in range(T):
            for step in range(1, C):
                place = crecv.at[n, tstep, slot, step - 1]
                remote(
                    place, place, oc_send.at[n, tstep, slot, step - 1],
                    oc_recv.at[n, tstep, slot, step - 1], "dp", (c + step) % C,
                ).wait_send()
        for tstep in range(T - 1):
            place = yrecv.at[n, tstep, slot]
            remote(
                place, place, oy_send.at[n, tstep, slot], oy_recv.at[n, tstep, slot],
                "tensor", (t + 1 + tstep) % T,
            ).wait_send()

        @pl.when(slot != a)
        def _():
            place = zrecv.at[n, slot]
            remote(
                place, place, oz_send.at[n, slot], oz_recv.at[n, slot],
                "fsdp", ((a + 1) % R) * S + b,
            ).wait_send()

        return carry

    lax.fori_loop(0, p.parts * R, settle, 0)
    for n in range(p.parts):
        write_out(n).wait()


def make_body(mesh):
    def body(states, fresh_rows, norm_gain, gate_weight, up_weight, down_weight, halted, refill_index):
        p = Plan(mesh, states, gate_weight, down_weight)
        R, S, T, C, K = p.R, p.S, p.T, p.C, p.K
        cap, width, fw, hp, pw = p.cap, p.width, p.fw, p.hp, p.pw
        bf16, f32 = jnp.bfloat16, jnp.float32
        dma = lambda *shape: pltpu.SemaphoreType.DMA(shape)
        vmem = pl.BlockSpec(memory_space=pltpu.VMEM)
        hbm = pl.BlockSpec(memory_space=pl.ANY)
        return pl.pallas_call(
            functools.partial(block_kernel, p),
            out_shape=jax.ShapeDtypeStruct(states.shape, states.dtype),
            in_specs=[vmem] * 3 + [hbm] * 5,
            out_specs=hbm,
            scratch_shapes=[
                pltpu.VMEM((p.rows, width), bf16),
                pltpu.VMEM((p.rows, width), bf16),
                pltpu.VMEM((p.rows, width), bf16),
                pltpu.VMEM((cap, p.rows), bf16),
                pltpu.VMEM((p.rows, cap), bf16),
                pltpu.VMEM((K, R, cap, width), bf16),
                pltpu.VMEM((p.features, hp), bf16),
                pltpu.VMEM((p.features, hp), bf16),
                pltpu.VMEM((p.halves, p.F, hp, pw), bf16),
                pltpu.VMEM((R, cap, hp), f32),
                pltpu.VMEM((R, cap, hp), f32),
                pltpu.VMEM((R, cap, hp), bf16),
                pltpu.VMEM((cap, width), bf16),
                pltpu.VMEM((C, cap, 128), f32),
                pltpu.VMEM((T, cap, 128), f32),
                pltpu.VMEM((p.parts, T, R, max(1, C - 1), cap, pw), bf16),
                pltpu.VMEM((p.parts, max(1, T - 1), R, cap, pw), bf16),
                pltpu.VMEM((p.parts, R + 1, cap, pw), bf16),
                pltpu.VMEM((p.parts, R, cap, pw), f32),
                dma(p.mats),
                dma(p.mats, R), dma(p.mats, R),
                dma(p.mats, R, S), dma(p.mats, R, S),
                dma(2, R), dma(R),
                dma(R, T), dma(R, T),
                dma(R, T, C), dma(R, T, C),
                dma(C), dma(C), dma(T), dma(T),
                dma(p.parts, T, R, max(1, C - 1)), dma(p.parts, T, R, max(1, C - 1)),
                dma(p.parts, max(1, T - 1), R), dma(p.parts, max(1, T - 1), R),
                dma(p.parts, R), dma(p.parts, R + 1),
                pltpu.SemaphoreType.REGULAR,
                dma(2), dma(p.parts),
            ],
            compiler_params=pltpu.CompilerParams(
                collective_id=0, has_side_effects=True, vmem_limit_bytes=64000 * 1024
            ),
        )(
            halted, refill_index, norm_gain, states, fresh_rows, gate_weight, up_weight, down_weight,
        )

    return body


def solution(mesh):
    columns = ("tensor", "dp")
    in_specs = (
        P("fsdp", columns),
        P("fsdp", columns),
        P(columns),
        P("fsdp", columns),
        P("fsdp", columns),
        P(columns, "fsdp"),
        P("fsdp", None),
        P("fsdp", None),
    )
    return jax.shard_map(
        make_body(mesh), mesh=mesh, in_specs=in_specs, out_specs=P("fsdp", columns), check_vma=False
    )
```

```python
import functools

import jax
import jax.numpy as jnp
from jax import lax
from jax.experimental import pallas as pl
from jax.experimental.pallas import tpu as pltpu
from jax.sharding import PartitionSpec as P

MESH = pl.DeviceIdType.MESH
norm_eps = 1e-05


class Plan:
    def __init__(self, mesh, states, gate, down):
        self.F, self.T, self.C = (mesh.shape[axis] for axis in ("fsdp", "tensor", "dp"))
        self.R = min(4, max(1, self.F // 2))
        self.S = self.F // self.R
        self.K = self.T * self.C
        self.unit = self.F // self.K
        self.rows, self.width = states.shape
        self.cap = self.rows * 3 // 4
        self.features = self.width * self.K
        self.fw = gate.shape[0]
        self.hp = gate.shape[1] // self.R
        self.halves = self.fw // 128
        self.pw = self.fw // self.halves
        self.gates, self.ups = [0, 1], [2, 3]
        self.down0 = 4
        self.mats = self.down0 + self.halves
        self.parts = self.unit * self.halves


def block_kernel(
    p,
    halted, refill, gain, states_in, fresh_in, gate_w, up_w, down_w,
    result,
    states, fresh, out, picker, spread,
    rows, gate_full, up_full, down_full, gate_acc, up_acc, hidden, kept, ms_c, ms_t,
    crecv, yrecv, zrecv, mine,
    local_sem, gz_send, gz_recv, xs_send, xs_recv, rz_send, rz_recv, ry_send, ry_recv,
    rc_send, rc_recv, mc_send, mc_recv, mt_send, mt_recv,
    oc_send, oc_recv, oy_send, oy_recv, oz_send, oz_recv, pair_sem, in_sem, out_sem,
):
    R, S, T, C, K = p.R, p.S, p.T, p.C, p.K
    cap, width, fw, hp, pw = p.cap, p.width, p.fw, p.hp, p.pw
    f, t, c = lax.axis_index("fsdp"), lax.axis_index("tensor"), lax.axis_index("dp")
    a, b = f // S, f % S
    me = t * C + c

    def remote(src, dst, send_sem, recv_sem, axis, index):
        return pltpu.make_async_remote_copy(
            src_ref=src, dst_ref=dst, send_sem=send_sem, recv_sem=recv_sem,
            device_id={axis: index}, device_id_type=MESH,
        )

    def when(cond, run):
        if cond is True:
            run()
        else:
            pl.when(cond)(run)

    def both(one, two):
        return two if one is True else jnp.logical_and(one, two)

    sent = []

    def send(make, cond=True, log=None):
        when(cond, lambda: make().start())
        (sent if log is None else log).append((make, cond))

    def near(step):
        return [(a - step, a >= step), (a + step, a + step < R)]

    by_distance = [(a, True)] + [pair for step in range(1, R) for pair in near(step)]
    arrivals = by_distance[1:]

    gates, ups, down0 = p.gates, p.ups, p.down0
    sub = fw // len(ups)

    def source_at(m, to):
        columns = pl.ds(pl.multiple_of(to * hp, hp), hp)
        if m < down0:
            k = m % len(ups)
            return (gate_w if m in gates else up_w).at[k * sub : (k + 1) * sub, columns]
        h = m - down0
        return down_w.at[columns, h * pw : (h + 1) * pw]

    def full_at(m, owner):
        if m < down0:
            span = pl.ds(pl.multiple_of(owner * fw + (m % len(ups)) * sub, sub), sub)
            return (gate_full if m in gates else up_full).at[span, :]
        return down_full.at[m - down0, owner]

    at_end = jnp.logical_or(a == 0, a == R - 1)

    def send_z(m, steps, where=None, choose=None):
        for step in steps:
            for to, cond in near(step):
                cond = cond if where is None else jnp.logical_and(cond, where)
                cond = cond if choose is None else jnp.logical_and(cond, choose(to))
                send(
                    lambda m=m, to=to: remote(
                        source_at(m, to), full_at(m, f), gz_send.at[m, to], gz_recv.at[m, a],
                        "fsdp", to * S + b,
                    ),
                    cond,
                )

    def wait_z(m, frm):
        place = full_at(m, frm * S + b)
        remote(place, place, gz_send.at[m, frm], gz_recv.at[m, frm], "fsdp", frm * S + b).wait_recv()

    def send_x(m, frm, cond, own=False):
        for step in range(1, S):
            def make(m=m, frm=frm, step=step):
                place = full_at(m, frm * S + b)
                return remote(
                    source_at(m, a) if own else place, place,
                    xs_send.at[m, frm, step], xs_recv.at[m, frm, step],
                    "fsdp", a * S + (b + step) % S,
                )
            send(make, cond)

    def wait_x(m, frm, step):
        owner = (b + S - step) % S
        place = full_at(m, frm * S + owner)
        remote(
            place, place, xs_send.at[m, frm, step], xs_recv.at[m, frm, step], "fsdp", a * S + owner
        ).wait_recv()

    def local(m):
        return pltpu.make_async_copy(source_at(m, a), full_at(m, f), local_sem.at[m])

    def forward_z(m, pairs):
        for frm, cond in pairs:
            when(cond, lambda frm=frm: wait_z(m, frm))
            send_x(m, frm, cond)

    fetch = [
        pltpu.make_async_copy(source, place, in_sem.at[k])
        for k, (source, place) in enumerate(((states_in, states), (fresh_in, fresh)))
    ]
    for copy in fetch:
        copy.start()
    barrier = pltpu.get_barrier_semaphore()
    partners = [("fsdp", ((a + step) % R) * S + b) for step in range(1, R)]
    partners += [("fsdp", a * S + (b + step) % S) for step in range(1, S)]
    partners += [("tensor", (t + step) % T) for step in range(1, T)]
    partners += [("dp", (c + step) % C) for step in range(1, C)]
    for axis, index in partners:
        pl.semaphore_signal(barrier, inc=1, device_id={axis: index}, device_id_type=MESH)
    pl.semaphore_wait(barrier, len(partners))

    far = list(range(2, R))
    close = range(1, min(R, 2))
    for m in gates:
        send_z(m, close)
    for m in gates:
        send_x(m, a, True, own=True)
    for m in range(p.mats):
        local(m).start()

    blocks, batch = halted.shape
    f32, bf16, i32 = jnp.float32, jnp.bfloat16, jnp.int32

    def ids(shape, axis):
        return lax.broadcasted_iota(i32, shape, axis)

    within = lax.rem(ids((batch, p.rows), 1), batch) == ids((batch, p.rows), 0)
    block_of = lax.div(ids((blocks, p.rows), 1), batch) == ids((blocks, p.rows), 0)

    def flat(table):
        wide = jnp.dot(table.astype(f32).astype(bf16), within.astype(bf16), preferred_element_type=f32)
        return jnp.sum(jnp.where(block_of, wide, 0.0), axis=0, keepdims=True)

    running = flat((halted[...] == 0).astype(i32))
    upto = (ids((p.rows, p.rows), 0) <= ids((p.rows, p.rows), 1)).astype(bf16)
    count = jnp.dot(jnp.broadcast_to(running, (8, p.rows)).astype(bf16), upto, preferred_element_type=f32)
    slot_row = jnp.where(running > 0.5, count[:1] - 1.0, -1.0).astype(i32)
    picker[...] = (ids((cap, p.rows), 0) == slot_row).astype(bf16)
    fetch[0].wait()
    picked = jnp.dot(picker[...], states[...], preferred_element_type=f32)
    kept[...] = picked.astype(jnp.bfloat16)
    ms_c[c] = jnp.broadcast_to(jnp.sum(picked * picked, axis=-1, keepdims=True), (cap, 128))

    def exchange(buffer, own, axis, count, send_sem, recv_sem):
        def copy(step):
            return remote(
                buffer.at[own], buffer.at[own], send_sem.at[step], recv_sem.at[step],
                axis, (own + step) % count,
            )
        for step in range(1, count):
            send(lambda step=step: copy(step))
        for step in range(1, count):
            place = buffer.at[(own + count - step) % count]
            remote(
                place, place, send_sem.at[step], recv_sem.at[step], axis, (own + count - step) % count
            ).wait_recv()
        return functools.reduce(lambda one, two: one + two, [buffer[k] for k in range(count)])

    ms_t[t] = exchange(ms_c, c, "dp", C, mc_send, mc_recv)
    total_square = exchange(ms_t, t, "tensor", T, mt_send, mt_recv)[:, :1]
    scale = lax.rsqrt(total_square / p.features + norm_eps)
    rows[me, a] = (
        kept[...].astype(jnp.float32) * scale * gain[...].astype(f32).reshape(1, width)
    ).astype(jnp.bfloat16)

    row_sent = []

    def row_z(slot, move, cond):
        way = 0 if move > 0 else 1
        place = lambda: rows.at[me, slot]
        send(
            lambda: remote(
                place(), place(), rz_send.at[way, slot], rz_recv.at[slot], "fsdp", (a + move) * S + b
            ),
            cond, row_sent,
        )

    def row_wait_z(slot):
        place = rows.at[me, slot]
        remote(place, place, rz_send.at[0, slot], rz_recv.at[slot], "fsdp", ((a + 1) % R) * S + b).wait_recv()

    def row_y(slot, cond):
        for step in range(1, T):
            send(
                lambda step=step: remote(
                    rows.at[me, slot], rows.at[me, slot], ry_send.at[slot, step], ry_recv.at[slot, step],
                    "tensor", (t + step) % T,
                ),
                cond, row_sent,
            )

    def row_c(slot, tstep, cond):
        block = ((t + T - tstep) % T) * C + c
        for step in range(1, C):
            send(
                lambda step=step: remote(
                    rows.at[block, slot], rows.at[block, slot],
                    rc_send.at[slot, tstep, step], rc_recv.at[slot, tstep, step],
                    "dp", (c + step) % C,
                ),
                cond, row_sent,
            )

    def row_step(step):
        for (slot, cond), move in zip(near(step), (1, -1)):
            when(cond, lambda slot=slot: row_wait_z(slot))
            more = (a + 1 < R) if move > 0 else (a > 0)
            row_z(slot, move, both(cond, more))
            row_y(slot, cond)
            row_c(slot, 0, cond)

    row_z(a, 1, a + 1 < R)
    row_z(a, -1, a > 0)
    for m in ups:
        send_z(m, close, at_end)
    row_y(a, True)
    row_c(a, 0, True)
    for m in range(len(gates), p.mats):
        send_x(m, a, True, own=True)

    base = lax.div(ids((1, p.rows), 1), batch) * batch
    fresh_row = jnp.where(running > 0.5, -1, flat(refill[...]).astype(i32) + base)
    filler = (ids((p.rows, p.rows), 0) == fresh_row).astype(bf16)
    turned = (((0,), (0,)), ((), ()))
    fetch[1].wait()
    out[...] = lax.dot_general(filler, fresh[...], turned, preferred_element_type=f32).astype(bf16)
    same = (ids((cap, cap), 0) == ids((cap, cap), 1)).astype(bf16)
    spread[...] = lax.dot_general(picker[...], same, turned, preferred_element_type=f32).astype(bf16)

    def row_arrive_y(pairs):
        for slot, cond in pairs:
            for tstep in range(1, T):
                place = lambda: rows.at[((t + T - tstep) % T) * C + c, slot]
                when(
                    cond,
                    lambda: remote(
                        place(), place(), ry_send.at[slot, tstep], ry_recv.at[slot, tstep],
                        "tensor", (t + T - tstep) % T,
                    ).wait_recv(),
                )
                row_c(slot, tstep, cond)

    inner = jnp.logical_not(at_end)
    beyond = range(3, R)

    def only(pairs, where):
        return [(frm, both(cond, where)) for frm, cond in pairs]

    def rim(pairs, yes):
        picked = []
        for frm, cond in pairs:
            end = jnp.logical_or(frm == 0, frm == R - 1)
            picked.append((frm, both(cond, end if yes else jnp.logical_not(end))))
        return picked

    for step in range(1, min(R, 3)):
        row_step(step)
        if step == 1:
            for m in gates:
                forward_z(m, near(1))
    for m in ups:
        send_z(m, close, inner, lambda to: jnp.logical_and(to > 0, to < R - 1))
    for m in gates:
        send_z(m, far, inner)
    for m in ups:
        send_z(m, far, inner)
    for m in gates:
        forward_z(m, only(near(2), at_end))
    for m in ups:
        forward_z(m, only(near(2), at_end))
    if C > 1:
        @pl.when(at_end)
        def _():
            for step in range(1, C):
                pl.semaphore_signal(
                    pair_sem, inc=1, device_id={"dp": (c + step) % C}, device_id_type=MESH
                )
            pl.semaphore_wait(pair_sem, C - 1)

    for m in (*gates, *ups):
        send_z(m, far[:1], at_end)
    for step in beyond:
        row_step(step)
    for m in (*gates, *ups):
        send_z(m, beyond, at_end)
    send_z(down0, close, at_end)
    send_z(down0, far, at_end)
    for h in range(1, p.halves):
        send_z(down0 + h, close, at_end)
    row_arrive_y(by_distance[:3])
    for m in ups:
        forward_z(m, only(near(1), inner))
    row_arrive_y(by_distance[3:])
    for m in ups:
        send_z(m, close, inner, lambda to: jnp.logical_or(to == 0, to == R - 1))
    for m in ups:
        forward_z(m, only(near(1), at_end))
    for m in gates:
        forward_z(m, only(near(2), inner))
    for slot in range(R):
        for tstep in range(T):
            for step in range(1, C):
                place = rows.at[((t + T - tstep) % T) * C + (c + C - step) % C, slot]
                remote(
                    place, place, rc_send.at[slot, tstep, step], rc_recv.at[slot, tstep, step],
                    "dp", (c + C - step) % C,
                ).wait_recv()
    for h in range(p.halves):
        send_z(down0 + h, close, inner)
        send_z(down0 + h, far, inner)

    per_owner = S // p.unit
    for m in range(p.mats):
        local(m).wait()

    def product_block(block, weights, acc, first):
        span = pl.ds(pl.multiple_of(block * width, width), width)

        def body(slot, carry):
            part = jnp.dot(rows[block, slot], weights[span, :], preferred_element_type=jnp.float32)
            acc[slot] = part if first else acc[slot] + part
            return carry

        lax.fori_loop(0, R, body, 0)

    def products(m, pairs):
        weights, acc = ((gate_full, gate_acc), (up_full, up_acc))[m]
        for frm, cond in pairs:
            def run(frm=frm, first=cond is True):
                for step in range(1, S):
                    for piece in ups if m else gates:
                        wait_x(piece, frm, step)
                for k in range(per_owner):
                    product_block(frm * per_owner + k, weights, acc, first and k == 0)
            when(cond, run)

    products(0, by_distance[:1])
    products(0, near(1))
    for m in ups:
        forward_z(m, only(near(2), inner))
    products(0, only(near(2), at_end))
    for step in beyond:
        for m in gates:
            forward_z(m, near(step))
    products(1, by_distance[:1])
    products(1, only(near(2), at_end))
    products(1, near(1))
    for step in beyond:
        for m in ups:
            forward_z(m, near(step))
        products(0, near(step))
    products(0, only(near(2), inner))
    products(1, only(near(2), inner))
    for step in beyond:
        products(1, near(step))

    def activate(slot, carry):
        gate = gate_acc[slot]
        hidden[slot] = (gate / (1.0 + jnp.exp(-gate)) * up_acc[slot]).astype(jnp.bfloat16)
        return carry

    lax.fori_loop(0, R, activate, 0)
    for make, cond in row_sent:
        when(cond, lambda make=make: make().wait_send())

    def slot_at(index):
        return jnp.where(index % 2 == 0, R - 1 - index // 2, index // 2)

    def column_part(n):
        return n // p.unit, (b + n % p.unit) % p.unit

    def product(n, slot, block):
        h, i = column_part(n)
        return jnp.dot(hidden[slot], down_full[h, block * p.unit + i], preferred_element_type=jnp.float32)

    def stage(n, block, slot):
        return rows.at[block, slot, :, n * pw : (n + 1) * pw]

    def out_c(n, tstep, slot, step):
        return remote(
            stage(n, tstep * (C - 1) + step - 1, slot), crecv.at[n, tstep, slot, step - 1],
            oc_send.at[n, tstep, slot, step - 1], oc_recv.at[n, tstep, slot, step - 1],
            "dp", (c + step) % C,
        )

    def out_y(n, tstep, slot):
        return remote(
            stage(n, T * (C - 1) + tstep, slot), yrecv.at[n, tstep, slot],
            oy_send.at[n, tstep, slot], oy_recv.at[n, tstep, slot],
            "tensor", (t + 1 + tstep) % T,
        )

    def out_z(n, slot):
        to = jnp.where(slot > a, a + 1, a - 1)
        land = jnp.where(slot == a - 1, R, slot)
        return remote(
            stage(n, K - 1, slot), zrecv.at[n, land], oz_send.at[n, slot], oz_recv.at[n, land],
            "fsdp", to * S + b,
        )

    def wait_out_z(n, land):
        place = zrecv.at[n, land]
        remote(place, place, oz_send.at[n, 0], oz_recv.at[n, land], "fsdp", ((a + 1) % R) * S + b).wait_recv()

    def part_a(n):
        h, turn = n // p.unit, n % p.unit
        m = down0 + h
        if turn == 0:
            forward_z(m, arrivals)
            if h + 1 < p.halves:
                send_z(m + 1, far, at_end)
        for frm in range(R):
            for step in range(1, S):
                if (step + turn) % p.unit == 0:
                    wait_x(m, frm, step)

    def part_a_products(n, low, high):
        def body(index, carry):
            tstep, slot = index // R, slot_at(index % R)
            for step in range(1, C):
                block = ((t + 1 + tstep) % T) * C + (c + step) % C
                place = stage(n, tstep * (C - 1) + step - 1, slot)
                place[...] = product(n, slot, block).astype(jnp.bfloat16)
                out_c(n, tstep, slot, step).start()
            return carry

        lax.fori_loop(low, high, body, 0)

    def chip_sum(n, tstep, slot):
        value = product(n, slot, ((t + 1 + tstep) % T) * C + c)
        for step in range(1, C):
            out_c(n, tstep, slot, step).wait_recv()
            value = value + crecv[n, tstep, slot, step - 1].astype(jnp.float32)
        return value

    def part_b(n, low, high):
        def body(index, carry):
            tstep, slot = index // (high - low), slot_at(low + index % (high - low))
            place = stage(n, T * (C - 1) + tstep, slot)
            place[...] = chip_sum(n, tstep, slot).astype(jnp.bfloat16)
            out_y(n, tstep, slot).start()
            return carry

        if high > low:
            lax.fori_loop(0, (T - 1) * (high - low), body, 0)

    def pass_on(n, slot, value):
        place = stage(n, K - 1, slot)
        place[...] = value.astype(jnp.bfloat16)
        out_z(n, slot).start()

    def part_c(n, low, high):
        def body(index, carry):
            slot = slot_at(index)
            value = chip_sum(n, T - 1, slot)
            for tstep in range(T - 1):
                out_y(n, tstep, slot).wait_recv()
                value = value + yrecv[n, tstep, slot].astype(jnp.float32)
            mine[n, slot] = value
            head = jnp.logical_or(
                jnp.logical_and(a == 0, slot > a), jnp.logical_and(a == R - 1, slot < a)
            )
            pl.when(head)(lambda: pass_on(n, slot, mine[n, slot]))
            return carry

        lax.fori_loop(low, high, body, 0)

    def part_s(n, low, high, hop):
        def body(index, carry):
            slot = slot_at(index)
            up = jnp.logical_and(a == hop, slot > a)
            down = jnp.logical_and(a == R - 1 - hop, slot < a)

            @pl.when(jnp.logical_or(up, down))
            def _():
                wait_out_z(n, slot)
                pass_on(n, slot, mine[n, slot] + zrecv[n, slot].astype(jnp.float32))

            return carry

        lax.fori_loop(low, high, body, 0)

    def part_f(n):
        for cond, land in ((a > 0, a), (a < R - 1, R)):
            @pl.when(cond)
            def _():
                wait_out_z(n, land)
                mine[n, a] = mine[n, a] + zrecv[n, land].astype(jnp.float32)

        h, i = column_part(n)
        columns = pl.ds(pl.multiple_of(i * fw + h * pw, pw), pw)
        settled = (kept[:, columns].astype(jnp.float32) + mine[n, a]).astype(jnp.bfloat16)
        placed = jnp.dot(spread[...], settled, preferred_element_type=jnp.float32)
        out[:, columns] = (placed + out[:, columns].astype(jnp.float32)).astype(jnp.bfloat16)
        write_out(n).start()

    def write_out(n):
        h, i = column_part(n)
        columns = pl.ds(pl.multiple_of(i * fw + h * pw, pw), pw)
        return pltpu.make_async_copy(out.at[:, columns], result.at[:, columns], out_sem.at[n])

    behind = 2
    for tick in range(p.parts + behind + R - 1):
        if tick < p.parts:
            part_a(tick)
            part_a_products(tick, 0, (T - 1) * R)
            part_b(tick, 0, R)
            part_a_products(tick, (T - 1) * R, T * R)
        if 0 <= tick - behind < p.parts:
            part_c(tick - behind, 0, R)
        for hop in range(1, R - 1):
            if 0 <= tick - behind + 1 - hop < p.parts:
                part_s(tick - behind + 1 - hop, 0, R, hop)
        if 0 <= tick - behind - R + 2 < p.parts:
            part_f(tick - behind - R + 2)

    for make, cond in sent:
        when(cond, lambda make=make: make().wait_send())

    def settle(index, carry):
        n, slot = index // R, index % R
        for tstep in range(T):
            for step in range(1, C):
                place = crecv.at[n, tstep, slot, step - 1]
                remote(
                    place, place, oc_send.at[n, tstep, slot, step - 1],
                    oc_recv.at[n, tstep, slot, step - 1], "dp", (c + step) % C,
                ).wait_send()
        for tstep in range(T - 1):
            place = yrecv.at[n, tstep, slot]
            remote(
                place, place, oy_send.at[n, tstep, slot], oy_recv.at[n, tstep, slot],
                "tensor", (t + 1 + tstep) % T,
            ).wait_send()

        @pl.when(slot != a)
        def _():
            place = zrecv.at[n, slot]
            remote(
                place, place, oz_send.at[n, slot], oz_recv.at[n, slot],
                "fsdp", ((a + 1) % R) * S + b,
            ).wait_send()

        return carry

    lax.fori_loop(0, p.parts * R, settle, 0)
    for n in range(p.parts):
        write_out(n).wait()


def make_body(mesh):
    def body(states, fresh_rows, norm_gain, gate_weight, up_weight, down_weight, halted, refill_index):
        p = Plan(mesh, states, gate_weight, down_weight)
        R, S, T, C, K = p.R, p.S, p.T, p.C, p.K
        cap, width, fw, hp, pw = p.cap, p.width, p.fw, p.hp, p.pw
        bf16, f32 = jnp.bfloat16, jnp.float32
        dma = lambda *shape: pltpu.SemaphoreType.DMA(shape)
        vmem = pl.BlockSpec(memory_space=pltpu.VMEM)
        hbm = pl.BlockSpec(memory_space=pl.ANY)
        return pl.pallas_call(
            functools.partial(block_kernel, p),
            out_shape=jax.ShapeDtypeStruct(states.shape, states.dtype),
            in_specs=[vmem] * 3 + [hbm] * 5,
            out_specs=hbm,
            scratch_shapes=[
                pltpu.VMEM((p.rows, width), bf16),
                pltpu.VMEM((p.rows, width), bf16),
                pltpu.VMEM((p.rows, width), bf16),
                pltpu.VMEM((cap, p.rows), bf16),
                pltpu.VMEM((p.rows, cap), bf16),
                pltpu.VMEM((K, R, cap, width), bf16),
                pltpu.VMEM((p.features, hp), bf16),
                pltpu.VMEM((p.features, hp), bf16),
                pltpu.VMEM((p.halves, p.F, hp, pw), bf16),
                pltpu.VMEM((R, cap, hp), f32),
                pltpu.VMEM((R, cap, hp), f32),
                pltpu.VMEM((R, cap, hp), bf16),
                pltpu.VMEM((cap, width), bf16),
                pltpu.VMEM((C, cap, 128), f32),
                pltpu.VMEM((T, cap, 128), f32),
                pltpu.VMEM((p.parts, T, R, max(1, C - 1), cap, pw), bf16),
                pltpu.VMEM((p.parts, max(1, T - 1), R, cap, pw), bf16),
                pltpu.VMEM((p.parts, R + 1, cap, pw), bf16),
                pltpu.VMEM((p.parts, R, cap, pw), f32),
                dma(p.mats),
                dma(p.mats, R), dma(p.mats, R),
                dma(p.mats, R, S), dma(p.mats, R, S),
                dma(2, R), dma(R),
                dma(R, T), dma(R, T),
                dma(R, T, C), dma(R, T, C),
                dma(C), dma(C), dma(T), dma(T),
                dma(p.parts, T, R, max(1, C - 1)), dma(p.parts, T, R, max(1, C - 1)),
                dma(p.parts, max(1, T - 1), R), dma(p.parts, max(1, T - 1), R),
                dma(p.parts, R), dma(p.parts, R + 1),
                pltpu.SemaphoreType.REGULAR,
                dma(2), dma(p.parts),
            ],
            compiler_params=pltpu.CompilerParams(
                collective_id=0, has_side_effects=True, vmem_limit_bytes=64000 * 1024
            ),
        )(
            halted, refill_index, norm_gain, states, fresh_rows, gate_weight, up_weight, down_weight,
        )

    return body


def solution(mesh):
    columns = ("tensor", "dp")
    in_specs = (
        P("fsdp", columns),
        P("fsdp", columns),
        P(columns),
        P("fsdp", columns),
        P("fsdp", columns),
        P(columns, "fsdp"),
        P("fsdp", None),
        P("fsdp", None),
    )
    return jax.shard_map(
        make_body(mesh), mesh=mesh, in_specs=in_specs, out_specs=P("fsdp", columns), check_vma=False
    )
```
